32 devices in a mesh: blk: 2 (over x), head: 4 (over z), weight: 4 (over y, core).
Axes of the slice: x: 2, y: 2, z: 4, core: 2. Of those that a mesh axis runs over, the one named last changes fastest.
Arguments:
- hidden_in: bfloat16 [2048, 2, 768], P(('blk', 'head', 'weight')), may hold values from -6 to 6
- qkv_weight: bfloat16 [768, 2304], replicated, may hold values from -0.21875 to 0.21875
- query_bias: float32 [768], replicated, may hold values from -3 to 3
- value_bias: float32 [768], replicated, may hold values from -0.12 to 0.12
- out_weight: bfloat16 [768, 768], replicated, may hold values from -5.75 to 5.75
- out_bias: float32 [768], replicated, may hold values from -3 to 3
- norm1_gain: float32 [768], replicated, may hold values from 0.25 to 1.75
- norm1_bias: float32 [768], replicated, may hold values from -3 to 3
- up_weight: bfloat16 [768, 3072], P(None, 'weight'), may hold values from -0.21875 to 0.21875
- up_bias: float32 [3072], P('weight'), may hold values from -3 to 3
- down_weight: bfloat16 [3072, 768], P('weight'), may hold values from -0.109375 to 0.109375
- down_bias: float32 [768], replicated, may hold values from -3 to 3
- norm2_gain: float32 [768], replicated, may hold values from 0.25 to 1.75
- norm2_bias: float32 [768], replicated, may hold values from -3 to 3
- lengths: int32 [2], replicated, may hold values from 256 to 2048, as said below
- out_cotangent: bfloat16 [2048, 2, 768], P(('blk', 'head', 'weight')), may hold values from -6 to 6
Outputs:
- layer_out: bfloat16 [2048, 2, 768], P(('blk', 'head', 'weight'))
- grad_in: float32 [2048, 2, 768], P(('blk', 'head', 'weight'))
- grad_qkv_weight: float32 [768, 2304], replicated
- grad_query_bias: float32 [768], replicated
- grad_value_bias: float32 [768], replicated
- grad_out_weight: float32 [768, 768], replicated
- grad_out_bias: float32 [768], replicated
- grad_norm1_gain: float32 [768], replicated
- grad_norm1_bias: float32 [768], replicated
- grad_up_weight: float32 [768, 3072], P(None, 'weight')
- grad_up_bias: float32 [3072], P('weight')
- grad_down_weight: float32 [3072, 768], P('weight')
- grad_down_bias: float32 [768], replicated
- grad_norm2_gain: float32 [768], replicated
- grad_norm2_bias: float32 [768], replicated
The draws below stay inside these ranges and needn't reach their ends.
Inputs may be any that keep to these rules, and one draw needn't show every extreme that they name: Positions 0 to lengths[b] - 1 of sequence b are tokens and the rest padding; at least one sequence has no padding.
All inputs are finite; a program needn't handle non-finite values.
Results may differ from the reference program's by a relative error of at most 0.02.
Values may be sent and summed in bfloat16 or wider, within the bound.
No kernel may reach another device: no remote copies, remote signals or barrier semaphores. Data moves between devices by JAX's collectives and lax.ppermute only.
A program may use at most 128 MiB of HBM per device.

```python
import math
import jax
import jax.numpy as jnp
from jax import lax

D = 768
HEADS = 12
FF = 3072
HEAD_DIM = 64
SEQS = 2
SEQ_LEN = 2048


def draw_lengths(key, part):
    base = jax.random.randint(jax.random.fold_in(key, 11), (SEQS,), SEQ_LEN // 8, SEQ_LEN + 1)
    chosen = jax.random.randint(jax.random.fold_in(key, 12), (), 0, SEQS)
    return jnp.where(jnp.arange(SEQS) == chosen, SEQ_LEN, base).astype(jnp.int32)


def level_of(key, shape, split, low, top_value):
    def one(position, blocks):
        steps = jax.random.uniform(jax.random.fold_in(jax.random.fold_in(key, 6), position), (blocks,), jnp.float32, low / len(split), top_value / len(split))
        return jnp.repeat(jnp.exp(steps), shape[position] // blocks).reshape((-1,) + (1,) * (len(shape) - position - 1))

    level = one(*split[0])
    for cut in split[1:]:
        level = level * one(*cut)
    return level


def scatter_about(key, extent, scale, reach, pieces=(), kind=jnp.bfloat16):
    values = jax.random.normal(key, extent, jnp.float32) * scale
    if len(pieces) > 0:
        values = level_of(key, extent, pieces, -0.22, 0.18) * values
    return jnp.clip(values, min=-reach, max=reach).astype(kind)


def setup_inputs(seed: int = 0) -> dict:
    splits = jax.random.split(jax.random.key(seed), 17)
    return {
        "hidden_in": scatter_about(splits[0], (SEQ_LEN, SEQS, D), 1.0, 6.0, ((0, 32),)),
        "qkv_weight": scatter_about(splits[1], (D, 3 * D), D ** -0.5, 0.21875),
        "query_bias": scatter_about(splits[2], (D,), 0.5, 3.0, (), jnp.float32),
        "value_bias": scatter_about(splits[3], (D,), 0.02, 0.12, (), jnp.float32),
        "out_weight": scatter_about(splits[4], (D, D), (0.68 * max(1, SEQ_LEN // D) ** 0.5), 5.75),
        "out_bias": scatter_about(splits[5], (D,), 0.5, 3.0, (), jnp.float32),
        "norm1_gain": jnp.clip(1.0 + 0.15 * jax.random.normal(splits[6], (D,), jnp.float32), 0.25, 1.75),
        "norm1_bias": scatter_about(splits[7], (D,), 0.5, 3.0, (), jnp.float32),
        "up_weight": scatter_about(splits[8], (D, FF), D ** -0.5, 0.21875, ((1, 4),)),
        "up_bias": scatter_about(splits[9], (FF,), 0.5, 3.0, ((0, 4),), jnp.float32),
        "down_weight": scatter_about(splits[10], (FF, D), FF ** -0.5, 0.109375, ((0, 4),)),
        "down_bias": scatter_about(splits[11], (D,), 0.5, 3.0, (), jnp.float32),
        "norm2_gain": jnp.clip(1.0 + 0.15 * jax.random.normal(splits[12], (D,), jnp.float32), 0.25, 1.75),
        "norm2_bias": scatter_about(splits[13], (D,), 0.5, 3.0, (), jnp.float32),
        "lengths": draw_lengths(jax.random.fold_in(splits[16], 71), 0),
        "out_cotangent": scatter_about(splits[15], (SEQ_LEN, SEQS, D), 1.0, 6.0, ((0, 32),)),
    }


EPS = 1e-05
SQRT_HALF = 0.7071067811865476
INV_ROOT_TAU = 0.3989422804014327

def norm_forward(resid, gain, bias):
    centre = lax.optimization_barrier(jnp.mean(resid, axis=-1, keepdims=True))
    centred = resid - centre
    spread = lax.optimization_barrier(jnp.mean(centred * centred, axis=-1, keepdims=True))
    rstd = lax.rsqrt(spread + EPS)
    normed = centred * rstd
    return (normed * gain + bias, normed, rstd)

def norm_backward(grad, normed, rstd, gain):
    scaled = grad * gain
    inner = scaled - lax.optimization_barrier(jnp.mean(scaled, axis=-1, keepdims=True)) - normed * lax.optimization_barrier(jnp.mean(scaled * normed, axis=-1, keepdims=True))
    return (rstd * inner, lax.optimization_barrier(jnp.sum(grad * normed, axis=0)), lax.optimization_barrier(jnp.sum(grad, axis=0)))

def gelu_value(pre):
    return 0.5 * pre * (1.0 + jax.scipy.special.erf(pre * SQRT_HALF))

def gelu_slope(pre):
    return 0.5 * (1.0 + jax.scipy.special.erf(pre * SQRT_HALF)) + pre * jnp.exp(-0.5 * pre * pre) * INV_ROOT_TAU

def block_rows():
    return math.gcd(SEQ_LEN, 512)

def attend_forward(query, keys, values, limit):
    scale = HEAD_DIM ** (-0.5)
    rows = block_rows()
    valid = jnp.arange(SEQ_LEN, dtype=jnp.int32) < limit
    keys_full = keys.astype(jnp.float32)
    values_full = values.astype(jnp.float32)
    blocks = query.reshape(SEQ_LEN // rows, rows, HEADS, HEAD_DIM)

    def single(qblock):
        scores = jnp.einsum('qhe,khe->hqk', qblock.astype(jnp.float32), keys_full) * scale
        weights = jnp.where(valid[None, None, :], jnp.exp(scores), 0.0)
        totals = lax.optimization_barrier(jnp.sum(weights, axis=-1))
        numer = jnp.einsum('hqk,khe->qhe', weights.astype(jnp.bfloat16).astype(jnp.float32), values_full)
        return ((numer / jnp.transpose(totals)[:, :, None]).astype(jnp.bfloat16), totals)
    outputs, totals = lax.map(single, blocks)
    return (outputs.reshape(SEQ_LEN, HEADS, HEAD_DIM), totals)

def attend_backward(query, keys, values, outputs, grad_out, totals, limit):
    scale = HEAD_DIM ** (-0.5)
    rows = block_rows()
    count = SEQ_LEN // rows
    valid = jnp.arange(SEQ_LEN, dtype=jnp.int32) < limit
    keys_full = keys.astype(jnp.float32)
    values_full = values.astype(jnp.float32)
    delta = lax.optimization_barrier(jnp.sum(grad_out.astype(jnp.float32) * outputs.astype(jnp.float32), axis=-1))
    qblocks = query.reshape(count, rows, HEADS, HEAD_DIM)
    gblocks = grad_out.reshape(count, rows, HEADS, HEAD_DIM)
    dblocks = delta.reshape(count, rows, HEADS)

    def single(carry, item):
        qblock, gblock, tblock, dblock = item
        qfull = qblock.astype(jnp.float32)
        gfull = gblock.astype(jnp.float32)
        scores = jnp.einsum('qhe,khe->hqk', qfull, keys_full) * scale
        weights = jnp.where(valid[None, None, :], jnp.exp(scores), 0.0)
        probs = weights / tblock[:, :, None]
        grad_prob = jnp.einsum('qhe,khe->hqk', gfull, values_full)
        grad_score = probs * (grad_prob - jnp.transpose(dblock)[:, :, None])
        score_half = grad_score.astype(jnp.bfloat16).astype(jnp.float32)
        value_part = jnp.einsum('hqk,qhe->khe', probs.astype(jnp.bfloat16).astype(jnp.float32), gfull)
        key_part = jnp.einsum('hqk,qhe->khe', score_half, qfull) * scale
        query_part = jnp.einsum('hqk,khe->qhe', score_half, keys_full) * scale
        return ((carry[0] + key_part, carry[1] + value_part), query_part)
    start = (jnp.zeros((SEQ_LEN, HEADS, HEAD_DIM), jnp.float32), jnp.zeros((SEQ_LEN, HEADS, HEAD_DIM), jnp.float32))
    (key_grad, value_grad), query_grad = lax.scan(single, start, (qblocks, gblocks, totals, dblocks))
    return (query_grad.reshape(SEQ_LEN, HEADS, HEAD_DIM), key_grad, value_grad)

def reference(hidden_in, qkv_weight, query_bias, value_bias, out_weight, out_bias, norm1_gain, norm1_bias, up_weight, up_bias, down_weight, down_bias, norm2_gain, norm2_bias, lengths, out_cotangent):
    tokens = SEQ_LEN * SEQS
    flat = hidden_in.reshape(tokens, D)
    bias_all = jnp.concatenate([query_bias, jnp.zeros((D,), jnp.float32), value_bias])
    packed = (jnp.dot(flat, qkv_weight, preferred_element_type=jnp.float32) + bias_all).astype(jnp.bfloat16)
    packed = packed.reshape(SEQ_LEN, SEQS, 3, HEADS, HEAD_DIM)
    outputs = []
    totals = []
    for member in range(SEQS):
        result, total = attend_forward(packed[:, member, 0], packed[:, member, 1], packed[:, member, 2], lengths[member])
        outputs.append(result)
        totals.append(total)
    attended = jnp.stack(outputs, axis=1).reshape(tokens, D)
    resid1 = flat.astype(jnp.float32) + jnp.dot(attended, out_weight, preferred_element_type=jnp.float32) + out_bias
    hidden1, normed1, rstd1 = norm_forward(resid1, norm1_gain, norm1_bias)
    hidden_half = hidden1.astype(jnp.bfloat16)
    pre = jnp.dot(hidden_half, up_weight, preferred_element_type=jnp.float32) + up_bias
    active = gelu_value(pre).astype(jnp.bfloat16)
    resid2 = hidden1 + jnp.dot(active, down_weight, preferred_element_type=jnp.float32) + down_bias
    final, normed2, rstd2 = norm_forward(resid2, norm2_gain, norm2_bias)
    layer_out = final.astype(jnp.bfloat16).reshape(SEQ_LEN, SEQS, D)
    cotangent = out_cotangent.reshape(tokens, D).astype(jnp.float32)
    grad_resid2, grad_norm2_gain, grad_norm2_bias = norm_backward(cotangent, normed2, rstd2, norm2_gain)
    grad_down_bias = lax.optimization_barrier(jnp.sum(grad_resid2, axis=0))
    grad_mixed = grad_resid2.astype(jnp.bfloat16)
    grad_down_weight = jnp.dot(active.T, grad_mixed, preferred_element_type=jnp.float32)
    grad_pre = jnp.dot(grad_mixed, down_weight.T, preferred_element_type=jnp.float32) * gelu_slope(pre)
    grad_up_bias = lax.optimization_barrier(jnp.sum(grad_pre, axis=0))
    grad_pre_half = grad_pre.astype(jnp.bfloat16)
    grad_up_weight = jnp.dot(hidden_half.T, grad_pre_half, preferred_element_type=jnp.float32)
    grad_hidden1 = grad_resid2 + jnp.dot(grad_pre_half, up_weight.T, preferred_element_type=jnp.float32)
    grad_resid1, grad_norm1_gain, grad_norm1_bias = norm_backward(grad_hidden1, normed1, rstd1, norm1_gain)
    grad_out_bias = lax.optimization_barrier(jnp.sum(grad_resid1, axis=0))
    grad_attn_half = grad_resid1.astype(jnp.bfloat16)
    grad_out_weight = jnp.dot(attended.T, grad_attn_half, preferred_element_type=jnp.float32)
    grad_attended = jnp.dot(grad_attn_half, out_weight.T, preferred_element_type=jnp.float32).astype(jnp.bfloat16)
    grad_attended = grad_attended.reshape(SEQ_LEN, SEQS, HEADS, HEAD_DIM)
    stacks = []
    for member in range(SEQS):
        query_grad, key_grad, value_grad = attend_backward(packed[:, member, 0], packed[:, member, 1], packed[:, member, 2], outputs[member], grad_attended[:, member], totals[member], lengths[member])
        stacks.append(jnp.stack([query_grad, key_grad, value_grad], axis=1))
    grad_packed = jnp.stack(stacks, axis=1).astype(jnp.bfloat16).reshape(tokens, 3 * D)
    grad_qkv_weight = jnp.dot(flat.T, grad_packed, preferred_element_type=jnp.float32)
    column_sums = lax.optimization_barrier(jnp.sum(grad_packed.astype(jnp.float32), axis=0))
    grad_query_bias = column_sums[:D]
    grad_value_bias = column_sums[2 * D:]
    grad_in = (jnp.dot(grad_packed, qkv_weight.T, preferred_element_type=jnp.float32) + grad_resid1).reshape(SEQ_LEN, SEQS, D)
    return (layer_out, grad_in, grad_qkv_weight, grad_query_bias, grad_value_bias, grad_out_weight, grad_out_bias, grad_norm1_gain, grad_norm1_bias, grad_up_weight, grad_up_bias, grad_down_weight, grad_down_bias, grad_norm2_gain, grad_norm2_bias)
```

```python
import jax
import jax.numpy as jnp
from jax import lax
from jax.experimental import pallas as pl
from jax.experimental.pallas import tpu as pltpu
from jax.sharding import PartitionSpec as P

HEADS = 12
HEAD_DIM = 64
EPS = 1e-05
SQRT_HALF = 0.7071067811865476
INV_ROOT_TAU = 0.3989422804014327
SCALE = HEAD_DIM ** (-0.5)
FAR = -1e30
F32 = jnp.float32
BF16 = jnp.bfloat16
NT = (((1,), (1,)), ((), ()))
TN = (((0,), (0,)), ((), ()))


def norm_forward(resid, gain, bias):
    centre = jnp.mean(resid, axis=-1, keepdims=True)
    centred = resid - centre
    spread = jnp.mean(centred * centred, axis=-1, keepdims=True)
    rstd = lax.rsqrt(spread + EPS)
    normed = centred * rstd
    return (normed * gain + bias, normed, rstd)


def norm_backward(grad, normed, rstd, gain):
    scaled = grad * gain
    inner = (
        scaled
        - jnp.mean(scaled, axis=-1, keepdims=True)
        - normed * jnp.mean(scaled * normed, axis=-1, keepdims=True)
    )
    return (rstd * inner, jnp.sum(grad * normed, axis=0), jnp.sum(grad, axis=0))


def gelu_value(pre):
    return 0.5 * pre * (1.0 + lax.erf(pre * SQRT_HALF))


def gelu_slope(pre):
    return 0.5 * (1.0 + lax.erf(pre * SQRT_HALF)) + pre * jnp.exp(-0.5 * pre * pre) * INV_ROOT_TAU


def lane_plan(heads):
    data = heads * HEAD_DIM
    wide = -(-(data + 1 + 6 * heads) // 128) * 128
    return data, wide, data + 1, data + 1 + 3 * heads


def head_lanes(heads, head):
    data, wide, delta_at, total_at = lane_plan(heads)
    lane = lax.broadcasted_iota(jnp.int32, (1, wide), 1)

    def within(start, count):
        return (lane >= start) & (lane < start + count)

    own = within(head * HEAD_DIM, HEAD_DIM)
    extra = (
        (lane == data)
        | within(delta_at + 3 * head, 3)
        | within(total_at + 3 * head, 3)
    )
    return own.astype(F32), (own | extra).astype(BF16)


def three_parts(value):
    high = value.astype(BF16).astype(F32)
    rest = value - high
    middle = rest.astype(BF16).astype(F32)
    return high, middle, rest - middle


def spread_parts(values, start, wide):
    lane = lax.broadcasted_iota(jnp.int32, (1, wide), 1)
    out = 0.0
    for head, value in enumerate(values):
        for part, piece in enumerate(three_parts(value)):
            out = out + jnp.where(lane == start + 3 * head + part, piece, 0.0)
    return out


def on_chip(kernel, out_shape, scratch=(), name=None):
    return pl.pallas_call(
        kernel,
        out_shape=out_shape,
        scratch_shapes=list(scratch),
        compiler_params=pltpu.CompilerParams(vmem_limit_bytes=56 * 1024 * 1024),
        name=name,
    )


def attend(packed, packed_all, heads):
    data, wide, _, total_at = lane_plan(heads)
    rows = packed.shape[0]
    keys = packed_all.shape[0]
    block = min(1024, keys)

    def kernel(own_ref, all_ref, out_ref, logs_ref, acc_ref):
        acc_ref[...] = jnp.zeros_like(acc_ref)
        query = own_ref[:, :wide]

        def step(index, _):
            at = pl.ds(pl.multiple_of(index * block, block), block)
            key = all_ref[at, wide : 2 * wide]
            value = all_ref[at, 2 * wide :]
            for head in range(heads):
                _, mask = head_lanes(heads, head)
                scores = lax.dot_general(query * mask, key, NT, preferred_element_type=F32)
                weights = jnp.exp(scores).astype(BF16)
                acc_ref[head] += jnp.dot(weights, value, preferred_element_type=F32)
            return 0

        lax.fori_loop(0, keys // block, step, 0)
        out = jnp.zeros((rows, wide), F32)
        logs = []
        for head in range(heads):
            own, _ = head_lanes(heads, head)
            part = acc_ref[head]
            total = part[:, data : data + 1]
            out = out + (part / total) * own
            logs.append(jnp.log(total))
        out_ref[...] = out.astype(BF16)
        logs_ref[...] = spread_parts(logs, total_at, wide).astype(BF16)

    shape = jax.ShapeDtypeStruct((rows, wide), BF16)
    return on_chip(
        kernel, (shape, shape), [pltpu.VMEM((heads, rows, wide), F32)], name="attend"
    )(packed, packed_all)


def output_grad(grad, out_own, attended, logs, heads):
    data, wide, delta_at, _ = lane_plan(heads)
    rows = grad.shape[0]

    def kernel(grad_ref, weight_ref, att_ref, logs_ref, out_ref):
        back = lax.dot_general(grad_ref[...], weight_ref[...], NT, preferred_element_type=F32)
        back = back.astype(BF16).astype(F32)
        prod = back * att_ref[...].astype(F32)
        deltas = []
        for head in range(heads):
            own, _ = head_lanes(heads, head)
            deltas.append(jnp.sum(prod * own, axis=-1, keepdims=True))
        out = back + spread_parts(deltas, delta_at, wide) + logs_ref[...].astype(F32)
        out_ref[...] = out.astype(BF16)

    return on_chip(kernel, jax.ShapeDtypeStruct((rows, wide), BF16), name="output_grad")(
        grad, out_own, attended, logs
    )


def attend_back(packed, back, packed_all, back_all, heads):
    data, wide, _, total_at = lane_plan(heads)
    rows = packed.shape[0]
    total_rows = packed_all.shape[0]
    block = min(1024, total_rows)

    def kernel(own_ref, back_ref, all_ref, back_all_ref, out_ref, dq_ref, dk_ref, dv_ref):
        dq_ref[...] = jnp.zeros_like(dq_ref)
        dk_ref[...] = jnp.zeros_like(dk_ref)
        dv_ref[...] = jnp.zeros_like(dv_ref)
        lane = lax.broadcasted_iota(jnp.int32, (1, wide), 1)
        logs = ((lane >= total_at) & (lane < total_at + 3 * heads)).astype(BF16)
        back_own = back_ref[...]
        query_own = own_ref[:, :wide] + back_own * logs
        key_own = own_ref[:, wide : 2 * wide]
        value_own = own_ref[:, 2 * wide :]

        def step(index, _):
            at = pl.ds(pl.multiple_of(index * block, block), block)
            key = all_ref[at, wide : 2 * wide]
            value = all_ref[at, 2 * wide :]
            back_in = back_all_ref[at, :]
            query_plain = all_ref[at, :wide]
            query = query_plain + back_in * logs
            for head in range(heads):
                _, mask = head_lanes(heads, head)
                scores = lax.dot_general(query_own * mask, key, NT, preferred_element_type=F32)
                inner = lax.dot_general(back_own * mask, value, NT, preferred_element_type=F32)
                half = (jnp.exp(scores) * inner).astype(BF16)
                dq_ref[head] += jnp.dot(half, key, preferred_element_type=F32)
                scores = lax.dot_general(key_own * mask, query, NT, preferred_element_type=F32)
                probs = jnp.exp(scores)
                inner = lax.dot_general(value_own * mask, back_in, NT, preferred_element_type=F32)
                half = (probs * inner).astype(BF16)
                dv_ref[head] += jnp.dot(probs.astype(BF16), back_in, preferred_element_type=F32)
                dk_ref[head] += jnp.dot(half, query_plain, preferred_element_type=F32)
            return 0

        lax.fori_loop(0, total_rows // block, step, 0)
        for slot, (ref, factor) in enumerate(((dq_ref, SCALE), (dk_ref, 1.0), (dv_ref, 1.0))):
            out = jnp.zeros((rows, wide), F32)
            for head in range(heads):
                own, _ = head_lanes(heads, head)
                out = out + ref[head] * (own * factor)
            out_ref[:, slot * wide : (slot + 1) * wide] = out.astype(BF16)

    acc = pltpu.VMEM((heads, rows, wide), F32)
    return on_chip(
        kernel,
        jax.ShapeDtypeStruct((rows, 3 * wide), BF16),
        [acc, acc, acc],
        name="attend_back",
    )(packed, back, packed_all, back_all)


def bits_of(axis):
    return [(axis, bit) for bit in range(lax.axis_size(axis).bit_length() - 1)]


def bit_value(place):
    axis, bit = place
    return (lax.axis_index(axis) >> bit) & 1


def trade(value, place):
    axis, bit = place
    return lax.ppermute(
        value, axis, [(i, i ^ (1 << bit)) for i in range(lax.axis_size(axis))]
    )


def halve(value, places):
    for place in places:
        half = value.shape[0] // 2
        mine = bit_value(place)
        send = lax.dynamic_slice_in_dim(value, (1 - mine) * half, half, 0).astype(BF16)
        keep = lax.dynamic_slice_in_dim(value, mine * half, half, 0)
        value = keep.astype(F32) + trade(send, place).astype(F32)
    return value


def double(value, place):
    other = trade(value, place)
    first = bit_value(place) == 0
    return jnp.stack([jnp.where(first, value, other), jnp.where(first, other, value)])


def scatter_weight(value):
    for place in bits_of("weight"):
        value = value.reshape((-1, 2) + value.shape[1:])
        mine = bit_value(place)
        send = lax.dynamic_index_in_dim(value, 1 - mine, 1, keepdims=False).astype(BF16)
        keep = lax.dynamic_index_in_dim(value, mine, 1, keepdims=False)
        value = keep + trade(send, place).astype(F32)
    return value[0]


def gather_keys(value):
    out = lax.all_gather(value, "weight", axis=0, tiled=True)
    pairs = lax.axis_size("blk") // 2
    pieces = [out]
    for hop in range(1, pairs):
        perm = [
            (2 * r + s, 2 * ((r + hop) % pairs) + s) for r in range(pairs) for s in range(2)
        ]
        pieces.append(lax.ppermute(out, "blk", perm))
    return out if len(pieces) == 1 else jnp.concatenate(pieces, axis=0)


def per_device(
    hidden_in,
    qkv_weight,
    query_bias,
    value_bias,
    out_weight,
    out_bias,
    norm1_gain,
    norm1_bias,
    up_weight,
    up_bias,
    down_weight,
    down_bias,
    norm2_gain,
    norm2_bias,
    lengths,
    out_cotangent,
):
    rows_here, _, width = hidden_in.shape
    head_devs = lax.axis_size("head")
    weight_devs = lax.axis_size("weight")
    blk = lax.axis_index("blk")
    head_at = lax.axis_index("head")
    weight_at = lax.axis_index("weight")
    seq = blk & 1
    first_seq = seq == 0
    heads = HEADS // head_devs
    data, wide, delta_at, total_at = lane_plan(heads)
    tokens = 2 * rows_here
    swap = ("blk", 0)

    def to_sequence(value):
        zero, one = value[:, 0], value[:, 1]
        mine = jnp.where(first_seq, zero, one)
        other = trade(jnp.where(first_seq, one, zero), swap)
        return jnp.concatenate([mine, other], axis=0)

    def from_sequence(value, narrow):
        mine = value[:rows_here]
        other = trade(value[rows_here:].astype(narrow), swap).astype(value.dtype)
        return jnp.stack(
            [jnp.where(first_seq, mine, other), jnp.where(first_seq, other, mine)], axis=1
        )

    flat = to_sequence(hidden_in)
    cotangent = to_sequence(out_cotangent).astype(F32)

    own = lax.dynamic_slice_in_dim(
        qkv_weight.reshape(width, 3, head_devs, data), head_at, 1, 2
    ).reshape(width, 3, data)
    factor = jnp.array([SCALE, 1.0, 1.0], F32)
    qkv_own = jnp.pad(
        own * factor.astype(BF16)[None, :, None], ((0, 0), (0, 0), (0, wide - data))
    ).reshape(width, 3 * wide)
    extra = jnp.zeros((3, wide), F32)
    extra = extra.at[0, data].set(1.0).at[2, data].set(1.0)
    extra = extra.at[2, delta_at : delta_at + 3 * heads].set(-1.0)
    extra = extra.at[1, total_at : total_at + 3 * heads].set(-1.0)
    bias_own = jnp.stack([
        lax.dynamic_slice_in_dim(query_bias, head_at * data, data) * SCALE,
        jnp.zeros((data,), F32),
        lax.dynamic_slice_in_dim(value_bias, head_at * data, data),
    ])
    bias_own = (jnp.pad(bias_own, ((0, 0), (0, wide - data))) + extra).reshape(1, 3 * wide)
    out_blocks = jnp.pad(
        out_weight.reshape(head_devs, data, width), ((0, 0), (0, wide - data), (0, 0))
    )
    out_own = lax.dynamic_index_in_dim(out_blocks, head_at, 0, keepdims=False)

    rows = lax.all_gather(flat, "head", axis=0, tiled=True)
    index = jnp.arange(head_devs * tokens, dtype=jnp.int32)
    source = index // tokens
    within = index % tokens
    source_blk = blk ^ (within // rows_here)
    position = (
        (source_blk * head_devs + source) * weight_devs + weight_at
    ) * rows_here + within % rows_here
    valid = position < jnp.where(first_seq, lengths[0], lengths[1])
    lane = jnp.arange(3 * wide, dtype=jnp.int32)
    masked = jnp.where((lane == wide + data)[None, :] & ~valid[:, None], FAR, 0.0)
    packed = (
        jnp.dot(rows, qkv_own, preferred_element_type=F32) + bias_own + masked
    ).astype(BF16)
    packed_all = gather_keys(packed)
    attended, logs = attend(packed, packed_all, heads)
    returned = lax.all_to_all(
        attended.reshape(head_devs, tokens, wide), "head", split_axis=0, concat_axis=0
    )
    resid1 = flat.astype(F32) + out_bias
    for group in range(head_devs):
        resid1 = resid1 + jnp.dot(
            returned[group], out_blocks[group], preferred_element_type=F32
        )
    hidden1, normed1, rstd1 = norm_forward(resid1, norm1_gain, norm1_bias)
    gathered = lax.all_gather(hidden1.astype(BF16), "weight", axis=0, tiled=True)
    pre = jnp.dot(gathered, up_weight, preferred_element_type=F32) + up_bias
    active = gelu_value(pre).astype(BF16)
    mixed = scatter_weight(
        jnp.dot(active, down_weight, preferred_element_type=F32).reshape(
            weight_devs, tokens, width
        )
    )
    resid2 = hidden1 + mixed + down_bias
    final, normed2, rstd2 = norm_forward(resid2, norm2_gain, norm2_bias)
    layer_out = from_sequence(final.astype(BF16), BF16)
    grad_resid2, grad_norm2_gain, grad_norm2_bias = norm_backward(
        cotangent, normed2, rstd2, norm2_gain
    )
    grad_down_bias = jnp.sum(grad_resid2, axis=0)
    mixed_all = lax.all_gather(grad_resid2.astype(BF16), "weight", axis=0, tiled=True)
    grad_pre = lax.dot_general(
        mixed_all, down_weight, NT, preferred_element_type=F32
    ) * gelu_slope(pre)
    grad_up_bias = jnp.sum(grad_pre, axis=0)
    grad_pre_half = grad_pre.astype(BF16)
    back_hidden = scatter_weight(
        lax.dot_general(grad_pre_half, up_weight, NT, preferred_element_type=F32).reshape(
            weight_devs, tokens, width
        )
    )
    grad_down_weight = lax.dot_general(active, mixed_all, TN, preferred_element_type=F32)
    grad_up_weight = lax.dot_general(gathered, grad_pre_half, TN, preferred_element_type=F32)
    grad_hidden1 = grad_resid2 + back_hidden
    grad_resid1, grad_norm1_gain, grad_norm1_bias = norm_backward(
        grad_hidden1, normed1, rstd1, norm1_gain
    )
    grad_out_bias = jnp.sum(grad_resid1, axis=0)
    grad_rows = lax.all_gather(grad_resid1.astype(BF16), "head", axis=0, tiled=True)
    back = output_grad(grad_rows, out_own, attended, logs, heads)
    back_all = gather_keys(back)
    grad_packed = attend_back(packed, back, packed_all, back_all, heads)

    grad_qkv_rows = lax.dot_general(grad_packed, rows, TN, preferred_element_type=F32)
    grad_out_rows = lax.dot_general(attended, grad_rows, TN, preferred_element_type=F32)
    stacked = jnp.concatenate(
        [grad_qkv_rows[at * wide : at * wide + data] for at in range(3)]
        + [grad_out_rows[:data]],
        axis=0,
    )
    weight_bits, blk_bits = bits_of("weight"), bits_of("blk")
    places = weight_bits + blk_bits
    piece = halve(stacked, places).astype(BF16)
    gathered_grads = lax.all_gather(piece, "head", axis=0)

    unscaled = jnp.repeat(jnp.array([1.0 / SCALE, 1.0, 1.0], F32), wide).astype(BF16)
    partial = lax.dot_general(
        grad_packed * unscaled, qkv_own, NT, preferred_element_type=F32
    ).astype(BF16)
    partial = lax.all_to_all(
        partial.reshape(head_devs, tokens, width), "head", split_axis=0, concat_axis=0
    )
    grad_in = jnp.sum(partial.astype(F32), axis=0) + grad_resid1
    grad_in = from_sequence(grad_in, BF16)

    column_sums = jnp.sum(grad_packed.astype(F32), axis=0).reshape(3, wide)[:, :data]
    blank = jnp.zeros((2, head_devs, data), F32)
    bias_rows = lax.dynamic_update_slice(
        blank, jnp.stack([column_sums[0], column_sums[2]])[:, None], (0, head_at, 0)
    ).reshape(2, width)
    small = jnp.concatenate(
        [
            bias_rows,
            jnp.stack([
                grad_out_bias,
                grad_norm1_gain,
                grad_norm1_bias,
                grad_norm2_gain,
                grad_norm2_bias,
                grad_down_bias,
            ]),
        ]
    )
    for place in places + bits_of("head"):
        small = small + trade(small, place)

    order = list(range(len(places)))
    half = width // 2

    def fan_out(value, first):
        held = []
        for at in first:
            value = double(value, places[at])
            held.insert(0, at)
        moved = [held.index(at) for at in order]
        count = len(held)
        value = jnp.transpose(value, (count, *moved, count + 1, count + 2))
        return value.reshape(head_devs, -1, half)

    core = order[:1]
    middle = order[1 : len(weight_bits)]
    outer = order[len(weight_bits) :]
    left = fan_out(gathered_grads[:, :, :half], outer + middle + core)
    right = fan_out(gathered_grads[:, :, half:], middle + outer + core)
    full = jnp.concatenate([left, right], axis=2)
    grad_qkv_weight = (
        jnp.transpose(full[:, : 3 * data].reshape(head_devs, 3, data, width), (3, 1, 0, 2))
        .reshape(width, 3 * width)
        .astype(F32)
    )
    grad_out_weight = full[:, 3 * data :].reshape(width, width).astype(F32)
    hidden_sums = lax.psum(
        (grad_up_weight.astype(BF16), grad_down_weight.astype(BF16)), ("blk", "head")
    )
    up_bias_sum = grad_up_bias.reshape(-1, 128)
    for place in blk_bits + bits_of("head"):
        up_bias_sum = up_bias_sum + trade(up_bias_sum, place)
    return (
        layer_out,
        grad_in,
        grad_qkv_weight,
        small[0],
        small[1],
        grad_out_weight,
        small[2],
        small[3],
        small[4],
        hidden_sums[0].astype(F32),
        up_bias_sum.reshape(-1),
        hidden_sums[1].astype(F32),
        small[7],
        small[5],
        small[6],
    )


def solution(mesh):
    placed = (
        P(("blk", "head", "weight"), None, None),
        P(),
        P(),
        P(),
        P(),
        P(),
        P(),
        P(),
        P(None, "weight"),
        P("weight"),
        P("weight", None),
        P(),
        P(),
        P(),
        P(),
        P(("blk", "head", "weight"), None, None),
    )
    return jax.shard_map(
        per_device,
        mesh=mesh,
        in_specs=placed,
        out_specs=(
            P(("blk", "head", "weight"), None, None),
            P(("blk", "head", "weight"), None, None),
            P(),
            P(),
            P(),
            P(),
            P(),
            P(),
            P(),
            P(None, "weight"),
            P("weight"),
            P("weight", None),
            P(),
            P(),
            P(),
        ),
        check_vma=False,
    )
```

```python
import jax
import jax.numpy as jnp
from jax import lax
from jax.experimental import pallas as pl
from jax.experimental.pallas import tpu as pltpu
from jax.sharding import PartitionSpec as P


HEADS = 12
HEAD_DIM = 64
EPS = 1e-05
SQRT_HALF = 0.7071067811865476
INV_ROOT_TAU = 0.3989422804014327
SCALE = HEAD_DIM ** (-0.5)
FAR = -1e30
F32 = jnp.float32
BF16 = jnp.bfloat16
NT = (((1,), (1,)), ((), ()))
TN = (((0,), (0,)), ((), ()))


def norm_forward(resid, gain, bias):
    centre = jnp.mean(resid, axis=-1, keepdims=True)
    centred = resid - centre
    spread = jnp.mean(centred * centred, axis=-1, keepdims=True)
    rstd = lax.rsqrt(spread + EPS)
    normed = centred * rstd
    return (normed * gain + bias, normed, rstd)


def norm_backward(grad, normed, rstd, gain):
    scaled = grad * gain
    inner = (
        scaled
        - jnp.mean(scaled, axis=-1, keepdims=True)
        - normed * jnp.mean(scaled * normed, axis=-1, keepdims=True)
    )
    return (rstd * inner, jnp.sum(grad * normed, axis=0), jnp.sum(grad, axis=0))


def gelu_value(pre):
    return 0.5 * pre * (1.0 + lax.erf(pre * SQRT_HALF))


def gelu_slope(pre):
    return 0.5 * (1.0 + lax.erf(pre * SQRT_HALF)) + pre * jnp.exp(-0.5 * pre * pre) * INV_ROOT_TAU


def lane_plan(heads):
    data = heads * HEAD_DIM
    wide = -(-(data + 1 + 6 * heads) // 128) * 128
    return data, wide, data + 1, data + 1 + 3 * heads


def head_lanes(heads, head):
    data, wide, delta_at, total_at = lane_plan(heads)
    lane = lax.broadcasted_iota(jnp.int32, (1, wide), 1)

    def within(start, count):
        return (lane >= start) & (lane < start + count)

    own = within(head * HEAD_DIM, HEAD_DIM)
    extra = (
        (lane == data)
        | within(delta_at + 3 * head, 3)
        | within(total_at + 3 * head, 3)
    )
    return own.astype(F32), (own | extra).astype(BF16)


def three_parts(value):
    high = value.astype(BF16).astype(F32)
    rest = value - high
    middle = rest.astype(BF16).astype(F32)
    return high, middle, rest - middle


def spread_parts(values, start, wide):
    lane = lax.broadcasted_iota(jnp.int32, (1, wide), 1)
    out = 0.0
    for head, value in enumerate(values):
        for part, piece in enumerate(three_parts(value)):
            out = out + jnp.where(lane == start + 3 * head + part, piece, 0.0)
    return out


def on_chip(kernel, out_shape, scratch=()):
    return pl.pallas_call(
        kernel,
        out_shape=out_shape,
        scratch_shapes=list(scratch),
        compiler_params=pltpu.CompilerParams(vmem_limit_bytes=56 * 1024 * 1024),
    )


def smem():
    return pl.BlockSpec(memory_space=pltpu.SMEM)


def vmem(count):
    return [pl.BlockSpec(memory_space=pltpu.VMEM)] * count


def prepare(qkv_weight, out_weight, query_bias, value_bias, head_at, head_devs):
    heads = HEADS // head_devs
    data, wide, delta_at, total_at = lane_plan(heads)
    width = qkv_weight.shape[0]

    def kernel(at_ref, qkv_ref, out_ref, qb_ref, vb_ref, q_ref, kv_ref, bias_ref, rows_ref):
        at = at_ref[0]
        pair = at // 2
        odd = (at - 2 * pair).astype(F32)
        lane = lax.broadcasted_iota(jnp.int32, (1, wide), 1)
        keep = (lane < data).astype(F32)

        def pick(value):
            high = pltpu.roll(value, data, 1)
            return (value * (1.0 - odd) + high * odd)[:, :wide] * keep

        def columns(group):
            start = pl.multiple_of(group * width + pair * 2 * data, 128)
            return pick(qkv_ref[:, pl.ds(start, 2 * data)].astype(F32))

        q_ref[...] = (columns(0) * SCALE).astype(BF16)
        kv_ref[:, :wide] = columns(1).astype(BF16)
        kv_ref[:, wide:] = columns(2).astype(BF16)
        start = pl.ds(pl.multiple_of(pair * 2 * data, 128), 2 * data)
        ones = (lane == data).astype(F32)
        deltas = ((lane >= delta_at) & (lane < delta_at + 3 * heads)).astype(F32)
        totals = ((lane >= total_at) & (lane < total_at + 3 * heads)).astype(F32)
        query = pick(jnp.broadcast_to(qb_ref[:, start], (8, 2 * data)))[:1]
        value = pick(jnp.broadcast_to(vb_ref[:, start], (8, 2 * data)))[:1]
        bias_ref[:, :wide] = query * SCALE + ones
        bias_ref[:, wide : 2 * wide] = -totals
        bias_ref[:, 2 * wide :] = value + ones - deltas
        for hop in range(head_devs):
            source = pl.multiple_of((at ^ hop) * data, HEAD_DIM)
            rows_ref[hop * wide : hop * wide + data] = out_ref[pl.ds(source, data), :]
            rows_ref[hop * wide + data : (hop + 1) * wide] = jnp.zeros(
                (wide - data, width), BF16
            )

    return pl.pallas_call(
        kernel,
        out_shape=(
            jax.ShapeDtypeStruct((width, wide), BF16),
            jax.ShapeDtypeStruct((width, 2 * wide), BF16),
            jax.ShapeDtypeStruct((1, 3 * wide), F32),
            jax.ShapeDtypeStruct((head_devs * wide, width), BF16),
        ),
        in_specs=[smem()] + vmem(4),
        compiler_params=pltpu.CompilerParams(vmem_limit_bytes=56 * 1024 * 1024),
        name="prepare",
    )(
        head_at.reshape(1),
        qkv_weight,
        out_weight,
        query_bias.reshape(1, width),
        value_bias.reshape(1, width),
    )


def attend(query, blocks, heads, pieces):
    data, wide, _, total_at = lane_plan(heads)
    rows = query.shape[0]
    size = rows // pieces
    count = len(blocks)

    def kernel(*refs):
        query_ref, block_refs = refs[0], refs[1 : 1 + count]
        out_ref, logs_ref = refs[1 + count : 3 + count]
        piece_refs, acc_ref = refs[3 + count : -1], refs[-1]
        query = query_ref[...]
        for index, ref in enumerate(block_refs):
            key = ref[:, :wide]
            value = ref[:, wide:]
            for head in range(heads):
                _, mask = head_lanes(heads, head)
                scores = lax.dot_general(query * mask, key, NT, preferred_element_type=F32)
                weights = jnp.exp(scores).astype(BF16)
                part = jnp.dot(weights, value, preferred_element_type=F32)
                acc_ref[head] = part if index == 0 else acc_ref[head] + part
        out = jnp.zeros((rows, wide), F32)
        logs = []
        for head in range(heads):
            own, _ = head_lanes(heads, head)
            part = acc_ref[head]
            total = part[:, data : data + 1]
            out = out + (part / total) * own
            logs.append(jnp.log(total))
        out = out.astype(BF16)
        out_ref[...] = out
        for index, ref in enumerate(piece_refs):
            ref[...] = out[index * size : (index + 1) * size]
        logs_ref[...] = spread_parts(logs, total_at, wide).astype(BF16)

    shape = jax.ShapeDtypeStruct((rows, wide), BF16)
    small = jax.ShapeDtypeStruct((size, wide), BF16)
    return on_chip(
        kernel, (shape, shape) + (small,) * pieces, [pltpu.VMEM((heads, rows, wide), F32)]
    )(query, *blocks)


def project_back(grad, out_rows, pieces):
    rows = grad.shape[0]
    wide = out_rows.shape[0] // pieces

    def kernel(grad_ref, weight_ref, *outs):
        for index, ref in enumerate(outs):
            weight = weight_ref[index * wide : (index + 1) * wide]
            ref[...] = lax.dot_general(
                grad_ref[...], weight, NT, preferred_element_type=F32
            ).astype(BF16)

    return on_chip(kernel, (jax.ShapeDtypeStruct((rows, wide), BF16),) * pieces)(grad, out_rows)


def with_stats(blocks, attended, logs, heads):
    _, wide, delta_at, _ = lane_plan(heads)
    size = blocks[0].shape[0]
    count = len(blocks)

    def kernel(*refs):
        att_ref, logs_ref, out_ref = refs[count:]
        for index, ref in enumerate(refs[:count]):
            at = slice(index * size, (index + 1) * size)
            back = ref[...].astype(F32)
            prod = back * att_ref[at].astype(F32)
            deltas = []
            for head in range(heads):
                own, _ = head_lanes(heads, head)
                deltas.append(jnp.sum(prod * own, axis=-1, keepdims=True))
            out = back + spread_parts(deltas, delta_at, wide) + logs_ref[at].astype(F32)
            out_ref[at] = out.astype(BF16)

    return on_chip(kernel, jax.ShapeDtypeStruct(attended.shape, BF16))(*blocks, attended, logs)


def add_to(ref, head, index, part):
    ref[head] = part if index == 0 else ref[head] + part


def merge_heads(ref, factor):
    heads, rows, wide = ref.shape
    out = jnp.zeros((rows, wide), F32)
    for head in range(heads):
        own, _ = head_lanes(heads, head)
        out = out + ref[head] * (own * factor)
    return out.astype(BF16)


def total_lanes(heads):
    _, wide, _, total_at = lane_plan(heads)
    lane = lax.broadcasted_iota(jnp.int32, (1, wide), 1)
    return ((lane >= total_at) & (lane < total_at + 3 * heads)).astype(BF16)


def query_side(query, back, keyvals, heads):
    _, wide, _, _ = lane_plan(heads)
    rows = query.shape[0]

    def kernel(query_ref, back_ref, *refs):
        keyval_refs, (out_ref, acc_ref) = refs[:-2], refs[-2:]
        back_own = back_ref[...]
        query_own = query_ref[...] + back_own * total_lanes(heads)
        for index, ref in enumerate(keyval_refs):
            key, value = ref[:, :wide], ref[:, wide:]
            for head in range(heads):
                _, mask = head_lanes(heads, head)
                scores = lax.dot_general(query_own * mask, key, NT, preferred_element_type=F32)
                inner = lax.dot_general(back_own * mask, value, NT, preferred_element_type=F32)
                half = (jnp.exp(scores) * inner).astype(BF16)
                add_to(acc_ref, head, index, jnp.dot(half, key, preferred_element_type=F32))
        out_ref[...] = merge_heads(acc_ref, SCALE)

    return on_chip(
        kernel, jax.ShapeDtypeStruct((rows, wide), BF16), [pltpu.VMEM((heads, rows, wide), F32)]
    )(query, back, *keyvals)


def key_side(own, queries, backs, heads):
    _, wide, _, _ = lane_plan(heads)
    rows = queries[0].shape[0]
    count = len(queries)

    def kernel(*refs):
        own_refs, refs = refs[: len(own)], refs[len(own) :]
        query_refs, back_refs = refs[:count], refs[count : 2 * count]
        out_ref, dk_ref, dv_ref = refs[2 * count :]
        keyval = jnp.concatenate([ref[...] for ref in own_refs])
        key_own, value_own = keyval[:, :wide], keyval[:, wide:]
        for index in range(count):
            back_in = back_refs[index][...]
            query_plain = query_refs[index][...]
            query = query_plain + back_in * total_lanes(heads)
            for head in range(heads):
                _, mask = head_lanes(heads, head)
                scores = lax.dot_general(key_own * mask, query, NT, preferred_element_type=F32)
                probs = jnp.exp(scores)
                inner = lax.dot_general(value_own * mask, back_in, NT, preferred_element_type=F32)
                half = (probs * inner).astype(BF16)
                part = jnp.dot(probs.astype(BF16), back_in, preferred_element_type=F32)
                add_to(dv_ref, head, index, part)
                part = jnp.dot(half, query_plain, preferred_element_type=F32)
                add_to(dk_ref, head, index, part)
        out_ref[:, :wide] = merge_heads(dk_ref, 1.0)
        out_ref[:, wide:] = merge_heads(dv_ref, 1.0)

    acc = pltpu.VMEM((heads, rows, wide), F32)
    return on_chip(
        kernel, jax.ShapeDtypeStruct((rows, 2 * wide), BF16), [acc, acc]
    )(*own, *queries, *backs)


def weight_rows(grad_query, grad_keyval, rows, attended, grad_rows, core, heads):
    data, wide, _, _ = lane_plan(heads)
    width = rows.shape[1]
    total = 4 * data

    def kernel(core_ref, dq_ref, dkv_ref, rows_ref, att_ref, grad_rows_ref, keep_ref, send_ref, sums_ref, all_ref):
        rows_in = rows_ref[...]
        for slot in range(3):
            part = dq_ref[...] if slot == 0 else dkv_ref[:, (slot - 1) * wide : slot * wide]
            out = lax.dot_general(part, rows_in, TN, preferred_element_type=F32)
            all_ref[slot * data : (slot + 1) * data] = out[:data]
            sums_ref[slot : slot + 1] = jnp.sum(part.astype(F32), axis=0, keepdims=True)
        out = lax.dot_general(
            att_ref[...], grad_rows_ref[...], TN, preferred_element_type=F32
        )
        all_ref[3 * data :] = out[:data]
        half = total // 2
        mine = pl.multiple_of(core_ref[0] * half, 64)
        theirs = pl.multiple_of((1 - core_ref[0]) * half, 64)
        keep_ref[...] = all_ref[pl.ds(mine, half), :]
        send_ref[...] = all_ref[pl.ds(theirs, half), :].astype(BF16)

    return pl.pallas_call(
        kernel,
        out_shape=(
            jax.ShapeDtypeStruct((total // 2, width), F32),
            jax.ShapeDtypeStruct((total // 2, width), BF16),
            jax.ShapeDtypeStruct((3, wide), F32),
        ),
        in_specs=[smem()] + vmem(5),
        scratch_shapes=[pltpu.VMEM((total, width), F32)],
        compiler_params=pltpu.CompilerParams(vmem_limit_bytes=56 * 1024 * 1024),
        name="weight_rows",
    )(core.reshape(1), grad_query, grad_keyval, rows, attended, grad_rows)


def input_rows(grad_query, grad_keyval, q_own, kv_own, pieces):
    width = q_own.shape[0]
    size = grad_query.shape[0] // pieces

    def kernel(dq_ref, dkv_ref, q_ref, kv_ref, *outs):
        query = (dq_ref[...].astype(F32) * (1.0 / SCALE)).astype(BF16)
        out = lax.dot_general(query, q_ref[...], NT, preferred_element_type=F32)
        out = out + lax.dot_general(
            dkv_ref[...], kv_ref[...], NT, preferred_element_type=F32
        )
        out = out.astype(BF16)
        for index, ref in enumerate(outs):
            ref[...] = out[index * size : (index + 1) * size]

    return on_chip(
        kernel, (jax.ShapeDtypeStruct((size, width), BF16),) * pieces
    )(grad_query, grad_keyval, q_own, kv_own)


def assemble(arrays, bits, plans, head_at, head_devs, heads):
    data, _, _, _ = lane_plan(heads)
    width = head_devs * data
    total = 4 * data
    size = total >> len(bits)

    def kernel(at_ref, *refs):
        ins, (qkv_ref, out_ref, all_ref) = refs[:4], refs[4:]
        own = [at_ref[index] for index in range(len(bits))]
        head = at_ref[len(bits)]
        for side, (halving, doubling) in enumerate(plans):
            lanes = slice(side * width // 2, (side + 1) * width // 2)
            for partner in range(2):
                ref = ins[2 * side + partner]
                for index in range(1 << len(doubling)):
                    flip = {place: (index >> at) & 1 for at, place in enumerate(doubling)}
                    start = (own[0] ^ partner) * (total // 2)
                    for level, place in enumerate(halving):
                        start = start + (own[place] ^ flip[place]) * (total >> (level + 2))
                    group = start // data
                    within = start - group * data
                    for hop in range(head_devs):
                        row = group * width + (head ^ hop) * data + within
                        from_row = (index * head_devs + hop) * size
                        all_ref[pl.ds(pl.multiple_of(row, 8), size), lanes] = ref[
                            from_row : from_row + size
                        ].astype(F32)
        out_ref[...] = all_ref[3 * width :]
        step = 256 if (3 * width) % 256 == 0 else 3 * width
        for start in range(0, 3 * width, step):
            qkv_ref[:, start : start + step] = all_ref[start : start + step].T

    return pl.pallas_call(
        kernel,
        out_shape=(
            jax.ShapeDtypeStruct((width, 3 * width), F32),
            jax.ShapeDtypeStruct((width, width), F32),
        ),
        in_specs=[smem()] + vmem(4),
        scratch_shapes=[pltpu.VMEM((4 * width, width), F32)],
        compiler_params=pltpu.CompilerParams(vmem_limit_bytes=56 * 1024 * 1024),
        name="assemble",
    )(jnp.stack(bits + [head_at]).astype(jnp.int32), *arrays)


def bits_of(axis):
    return [(axis, bit) for bit in range(lax.axis_size(axis).bit_length() - 1)]


def bit_value(place):
    axis, bit = place
    return (lax.axis_index(axis) >> bit) & 1


def hop(value, axis, distance):
    return lax.ppermute(value, axis, [(i, i ^ distance) for i in range(lax.axis_size(axis))])


def trade(value, place):
    return hop(value, place[0], 1 << place[1])


def after(value, *others):
    return lax.optimization_barrier((value, *others))[0]


def spread(value):
    high = lax.reduce_precision(value, 8, 7)
    return jnp.concatenate([high, value - high]).astype(BF16)


def halve_message(value, extra, place):
    half = value.shape[0] // 2
    mine = bit_value(place)
    send = lax.dynamic_slice_in_dim(value, (1 - mine) * half, half, 0).astype(BF16)
    keep = lax.dynamic_slice_in_dim(value, mine * half, half, 0)
    return jnp.concatenate([send, spread(extra)]), keep


def halve(value, extra, place):
    message, keep = halve_message(value, extra, place)
    return settle(keep, extra, trade(message, place))


def double(value, place):
    other = trade(value, place)
    first = bit_value(place) == 0
    return jnp.concatenate([jnp.where(first, value, other), jnp.where(first, other, value)])


def settle(keep, extra, got):
    half, count = keep.shape[0], extra.shape[0]
    got = got.astype(F32)
    return (
        keep + got[:half],
        extra + got[half : half + count] + got[half + count :],
    )


def scatter_weight(value):
    for place in bits_of("weight"):
        value = value.reshape((-1, 2) + value.shape[1:])
        mine = bit_value(place)
        send = lax.dynamic_index_in_dim(value, 1 - mine, 1, keepdims=False).astype(BF16)
        keep = lax.dynamic_index_in_dim(value, mine, 1, keepdims=False)
        value = keep + trade(send, place).astype(F32)
    return value[0]


def gather_blocks(value):
    blocks = [value]
    for place in bits_of("weight")[::-1] + bits_of("blk")[1:]:
        blocks = blocks + [trade(block, place) for block in blocks]
    return blocks


def per_device(
    hidden_in,
    qkv_weight,
    query_bias,
    value_bias,
    out_weight,
    out_bias,
    norm1_gain,
    norm1_bias,
    up_weight,
    up_bias,
    down_weight,
    down_bias,
    norm2_gain,
    norm2_bias,
    lengths,
    out_cotangent,
):
    rows_here, _, width = hidden_in.shape
    head_devs = lax.axis_size("head")
    weight_devs = lax.axis_size("weight")
    blk = lax.axis_index("blk")
    head_at = lax.axis_index("head")
    weight_at = lax.axis_index("weight")
    first_seq = (blk & 1) == 0
    heads = HEADS // head_devs
    data, wide, _, _ = lane_plan(heads)
    tokens = 2 * rows_here
    swap = ("blk", 0)

    def to_sequence(value):
        zero, one = value[:, 0], value[:, 1]
        mine = jnp.where(first_seq, zero, one)
        other = trade(jnp.where(first_seq, one, zero), swap)
        return jnp.concatenate([mine, other], axis=0)

    def from_sequence(value, narrow):
        mine = value[:rows_here]
        other = trade(value[rows_here:].astype(narrow), swap).astype(value.dtype)
        return jnp.stack(
            [jnp.where(first_seq, mine, other), jnp.where(first_seq, other, mine)], axis=1
        )

    flat = to_sequence(hidden_in)
    q_own, kv_own, bias_own, out_rows = prepare(
        after(qkv_weight, flat), out_weight, query_bias, value_bias, head_at, head_devs
    )
    hops = [flat] + [hop(flat, "head", at) for at in range(1, head_devs)]
    split = head_devs // 2
    near, far = jnp.concatenate(hops[:split]), jnp.concatenate(hops[split:])
    cotangent = to_sequence(after(out_cotangent, flat)).astype(F32)

    def project(part, first):
        index = jnp.arange(part.shape[0], dtype=jnp.int32)
        source = head_at ^ (first + index // tokens)
        within = index % tokens
        source_blk = blk ^ (within // rows_here)
        position = (
            (source_blk * head_devs + source) * weight_devs + weight_at
        ) * rows_here + within % rows_here
        valid = position < jnp.where(first_seq, lengths[0], lengths[1])
        lane = jnp.arange(2 * wide, dtype=jnp.int32)
        masked = jnp.where((lane == data)[None, :] & ~valid[:, None], FAR, 0.0)
        return (
            jnp.dot(part, kv_own, preferred_element_type=F32) + bias_own[:, wide:] + masked
        ).astype(BF16)

    own_keyvals = [project(near, 0), project(far, split)]
    keyvals = gather_blocks(own_keyvals[0])
    keyvals = keyvals + gather_blocks(own_keyvals[1])
    rows = jnp.concatenate([near, far])
    query = (
        jnp.dot(rows, q_own, preferred_element_type=F32) + bias_own[:, :wide]
    ).astype(BF16)
    attended, logs, *parts = attend(query, keyvals, heads, head_devs)
    queries = gather_blocks(after(query, attended))
    returned = [parts[0]] + [hop(parts[at], "head", at) for at in range(1, head_devs)]
    returned = jnp.concatenate(returned, axis=1)
    resid1 = flat.astype(F32) + jnp.dot(returned, out_rows, preferred_element_type=F32) + out_bias
    hidden1, normed1, rstd1 = norm_forward(resid1, norm1_gain, norm1_bias)
    gathered = lax.all_gather(hidden1.astype(BF16), "weight", axis=0, tiled=True)
    pre = jnp.dot(gathered, up_weight, preferred_element_type=F32) + up_bias
    active = gelu_value(pre).astype(BF16)
    mixed = scatter_weight(
        jnp.dot(active, down_weight, preferred_element_type=F32).reshape(
            weight_devs, tokens, width
        )
    )
    resid2 = hidden1 + mixed + down_bias
    final, normed2, rstd2 = norm_forward(resid2, norm2_gain, norm2_bias)
    grad_resid2, grad_norm2_gain, grad_norm2_bias = norm_backward(
        cotangent, normed2, rstd2, norm2_gain
    )
    grad_down_bias = jnp.sum(grad_resid2, axis=0)
    mixed_all = lax.all_gather(grad_resid2.astype(BF16), "weight", axis=0, tiled=True)
    grad_pre = lax.dot_general(
        mixed_all, down_weight, NT, preferred_element_type=F32
    ) * gelu_slope(pre)
    grad_up_bias = jnp.sum(grad_pre, axis=0)
    grad_pre_half = grad_pre.astype(BF16)
    back_hidden = scatter_weight(
        lax.dot_general(grad_pre_half, up_weight, NT, preferred_element_type=F32).reshape(
            weight_devs, tokens, width
        )
    )
    grad_down_weight = lax.dot_general(active, mixed_all, TN, preferred_element_type=F32)
    grad_up_weight = lax.dot_general(gathered, grad_pre_half, TN, preferred_element_type=F32)
    up_extra = jnp.pad(grad_up_bias[None], ((0, 7), (0, 0)))
    ffn_keep = jnp.where(first_seq, grad_up_weight, grad_down_weight)
    ffn_send = jnp.concatenate(
        [
            jnp.where(first_seq, grad_down_weight, grad_up_weight).astype(BF16),
            spread(up_extra),
        ]
    )
    grad_hidden1 = grad_resid2 + back_hidden
    grad_resid1, grad_norm1_gain, grad_norm1_bias = norm_backward(
        grad_hidden1, normed1, rstd1, norm1_gain
    )
    grad_out_bias = jnp.sum(grad_resid1, axis=0)
    grad_half, ffn_keep, ffn_send = lax.optimization_barrier(
        (grad_resid1.astype(BF16), ffn_keep, ffn_send)
    )
    ffn_got = trade(ffn_send, swap)
    ffn_places = bits_of("blk")[1:] + bits_of("head")
    layer_out = from_sequence(after(final.astype(BF16), grad_half), BF16)
    backs = project_back(grad_half, out_rows, head_devs)
    backs = [backs[0]] + [hop(backs[at], "head", at) for at in range(1, head_devs)]
    back = with_stats(backs, attended, logs, heads)
    back_blocks = gather_blocks(back)
    grad_late = after(grad_half, back)
    grad_rows = jnp.concatenate(
        [grad_late] + [hop(grad_late, "head", at) for at in range(1, head_devs)]
    )
    grad_query = query_side(query, back, keyvals, heads)
    ffn, up_extra = settle(ffn_keep, up_extra, after(ffn_got, grad_query))
    ffn_message, ffn_keep = halve_message(ffn, up_extra, ffn_places[0])
    ffn_got = trade(ffn_message, ffn_places[0])
    grad_keyval = key_side(own_keyvals, queries, back_blocks, heads)
    ffn, up_extra = settle(ffn_keep, up_extra, after(ffn_got, grad_keyval))
    for place in ffn_places[1:]:
        ffn, up_extra = halve(ffn, up_extra, place)
    ffn = ffn.astype(BF16)

    weight_bits, blk_bits = bits_of("weight"), bits_of("blk")
    core, middle, outer = weight_bits[0], weight_bits[1:], blk_bits
    keep, send, column_sums = weight_rows(
        grad_query, grad_keyval, rows, attended, grad_rows, bit_value(core), heads
    )
    column_sums = column_sums[:, :data]
    bias_rows = lax.dynamic_update_slice(
        jnp.zeros((2, head_devs, data), F32),
        jnp.stack([column_sums[0], column_sums[2]])[:, None],
        (0, head_at, 0),
    ).reshape(2, width)
    extra = jnp.concatenate(
        [
            bias_rows,
            jnp.stack([
                grad_out_bias,
                grad_norm1_gain,
                grad_norm1_bias,
                grad_norm2_gain,
                grad_norm2_bias,
                grad_down_bias,
            ]),
        ]
    )
    count = extra.shape[0]
    got = trade(jnp.concatenate([send, spread(extra)]), core)
    value, extra = settle(keep, extra, got)
    lane_half = width // 2
    orders = (middle + outer, outer + middle)
    sides = [
        (value[:, at * lane_half : (at + 1) * lane_half], extra[:, at * lane_half : (at + 1) * lane_half])
        for at in range(2)
    ]
    for level in range(len(middle + outer)):
        out = [halve_message(*sides[at], orders[at][level]) for at in range(2)]
        messages = lax.optimization_barrier((out[0][0], out[1][0]))
        got = [trade(messages[at], orders[at][level]) for at in range(2)]
        sides = [settle(out[at][1], sides[at][1], got[at]) for at in range(2)]
    sides = [jnp.concatenate([part.astype(BF16), spread(small)]) for part, small in sides]
    piece = jnp.concatenate(sides, axis=1)
    partial = input_rows(grad_query, grad_keyval, q_own, kv_own, head_devs)
    piece, *partial = lax.optimization_barrier((piece, *partial))
    pieces = [piece] + [hop(piece, "head", at) for at in range(1, head_devs)]
    size = piece.shape[0] - 2 * count
    small = sum(
        each[size : size + count].astype(F32) + each[size + count :].astype(F32)
        for each in pieces
    )
    stacked = jnp.concatenate([each[:size] for each in pieces])
    for place in ffn_places[::-1]:
        ffn = double(ffn, place)
    ffn_other = trade(ffn, swap)
    arrays, plans = [], []
    slot = {place: at for at, place in enumerate([core] + middle + outer)}
    for side, order in enumerate(orders):
        part = stacked[:, side * lane_half : (side + 1) * lane_half]
        for place in order[::-1]:
            part = jnp.concatenate([part, trade(part, place)])
        arrays += [part, trade(part, core)]
        plans.append(([slot[at] for at in order], [slot[at] for at in order[::-1]]))
    grad_qkv_weight, grad_out_weight = assemble(
        arrays,
        [bit_value(place) for place in [core] + middle + outer],
        plans,
        head_at,
        head_devs,
        heads,
    )

    partial = lax.optimization_barrier((*partial, stacked))[:-1]
    grad_in = grad_resid1 + partial[0].astype(F32)
    for at in range(1, head_devs):
        part = hop(partial[at], "head", at)
        grad_in = grad_in + part.astype(F32)
    grad_in = from_sequence(grad_in, BF16)
    return (
        layer_out,
        grad_in,
        grad_qkv_weight,
        small[0],
        small[1],
        grad_out_weight,
        small[2],
        small[3],
        small[4],
        jnp.where(first_seq, ffn, ffn_other).astype(F32),
        up_extra[0],
        jnp.where(first_seq, ffn_other, ffn).astype(F32),
        small[7],
        small[5],
        small[6],
    )


def solution(mesh):
    placed = (
        P(("blk", "head", "weight"), None, None),
        P(),
        P(),
        P(),
        P(),
        P(),
        P(),
        P(),
        P(None, "weight"),
        P("weight"),
        P("weight", None),
        P(),
        P(),
        P(),
        P(),
        P(("blk", "head", "weight"), None, None),
    )

    return jax.shard_map(
        per_device,
        mesh=mesh,
        in_specs=placed,
        out_specs=(
            P(("blk", "head", "weight"), None, None),
            P(("blk", "head", "weight"), None, None),
            P(),
            P(),
            P(),
            P(),
            P(),
            P(),
            P(),
            P(None, "weight"),
            P("weight"),
            P("weight", None),
            P(),
            P(),
            P(),
        ),
        check_vma=False,
    )
```

```python
import jax
import jax.numpy as jnp
from jax import lax
from jax.experimental import pallas as pl
from jax.experimental.pallas import tpu as pltpu
from jax.sharding import PartitionSpec as P


HEADS = 12
HEAD_DIM = 64
EPS = 1e-05
SQRT_HALF = 0.7071067811865476
INV_ROOT_TAU = 0.3989422804014327
SCALE = HEAD_DIM ** (-0.5)
FAR = -1e30
F32 = jnp.float32
BF16 = jnp.bfloat16
NT = (((1,), (1,)), ((), ()))
TN = (((0,), (0,)), ((), ()))


def norm_forward(resid, gain, bias):
    centre = jnp.mean(resid, axis=-1, keepdims=True)
    centred = resid - centre
    spread = jnp.mean(centred * centred, axis=-1, keepdims=True)
    rstd = lax.rsqrt(spread + EPS)
    normed = centred * rstd
    return (normed * gain + bias, normed, rstd)


def norm_backward(grad, normed, rstd, gain):
    scaled = grad * gain
    inner = (
        scaled
        - jnp.mean(scaled, axis=-1, keepdims=True)
        - normed * jnp.mean(scaled * normed, axis=-1, keepdims=True)
    )
    return (rstd * inner, jnp.sum(grad * normed, axis=0), jnp.sum(grad, axis=0))


def gelu_value(pre):
    return 0.5 * pre * (1.0 + lax.erf(pre * SQRT_HALF))


def gelu_slope(pre):
    return 0.5 * (1.0 + lax.erf(pre * SQRT_HALF)) + pre * jnp.exp(-0.5 * pre * pre) * INV_ROOT_TAU


def lane_plan(heads):
    data = heads * HEAD_DIM
    wide = -(-(data + 1 + 6 * heads) // 128) * 128
    return data, wide, data + 1, data + 1 + 3 * heads


def head_lanes(heads, head):
    data, wide, delta_at, total_at = lane_plan(heads)
    lane = lax.broadcasted_iota(jnp.int32, (1, wide), 1)

    def within(start, count):
        return (lane >= start) & (lane < start + count)

    own = within(head * HEAD_DIM, HEAD_DIM)
    extra = (
        (lane == data)
        | within(delta_at + 3 * head, 3)
        | within(total_at + 3 * head, 3)
    )
    return own.astype(F32), (own | extra).astype(BF16)


def three_parts(value):
    high = value.astype(BF16).astype(F32)
    rest = value - high
    middle = rest.astype(BF16).astype(F32)
    return high, middle, rest - middle


def spread_parts(values, start, wide):
    lane = lax.broadcasted_iota(jnp.int32, (1, wide), 1)
    out = 0.0
    for head, value in enumerate(values):
        for part, piece in enumerate(three_parts(value)):
            out = out + jnp.where(lane == start + 3 * head + part, piece, 0.0)
    return out


def on_chip(kernel, out_shape, scratch=()):
    return pl.pallas_call(
        kernel,
        out_shape=out_shape,
        scratch_shapes=list(scratch),
        compiler_params=pltpu.CompilerParams(vmem_limit_bytes=56 * 1024 * 1024),
    )


def smem():
    return pl.BlockSpec(memory_space=pltpu.SMEM)


def vmem(count):
    return [pl.BlockSpec(memory_space=pltpu.VMEM)] * count


def prepare(qkv_weight, out_weight, query_bias, value_bias, head_at, head_devs):
    heads = HEADS // head_devs
    data, wide, delta_at, total_at = lane_plan(heads)
    width = qkv_weight.shape[0]

    def kernel(at_ref, qkv_ref, out_ref, qb_ref, vb_ref, q_ref, kv_ref, bias_ref, rows_ref):
        at = at_ref[0]
        pair = at // 2
        odd = (at - 2 * pair).astype(F32)
        lane = lax.broadcasted_iota(jnp.int32, (1, wide), 1)
        keep = (lane < data).astype(F32)

        def pick(value):
            high = pltpu.roll(value, data, 1)
            return (value * (1.0 - odd) + high * odd)[:, :wide] * keep

        def columns(group):
            start = pl.multiple_of(group * width + pair * 2 * data, 128)
            return pick(qkv_ref[:, pl.ds(start, 2 * data)].astype(F32))

        q_ref[...] = (columns(0) * SCALE).astype(BF16)
        kv_ref[:, :wide] = columns(1).astype(BF16)
        kv_ref[:, wide:] = columns(2).astype(BF16)
        start = pl.ds(pl.multiple_of(pair * 2 * data, 128), 2 * data)
        ones = (lane == data).astype(F32)
        deltas = ((lane >= delta_at) & (lane < delta_at + 3 * heads)).astype(F32)
        totals = ((lane >= total_at) & (lane < total_at + 3 * heads)).astype(F32)
        query = pick(jnp.broadcast_to(qb_ref[:, start], (8, 2 * data)))[:1]
        value = pick(jnp.broadcast_to(vb_ref[:, start], (8, 2 * data)))[:1]
        bias_ref[:, :wide] = query * SCALE + ones
        bias_ref[:, wide : 2 * wide] = -totals
        bias_ref[:, 2 * wide :] = value + ones - deltas
        for hop in range(head_devs):
            source = pl.multiple_of((at ^ hop) * data, HEAD_DIM)
            rows_ref[hop * wide : hop * wide + data] = out_ref[pl.ds(source, data), :]
            rows_ref[hop * wide + data : (hop + 1) * wide] = jnp.zeros(
                (wide - data, width), BF16
            )

    return pl.pallas_call(
        kernel,
        out_shape=(
            jax.ShapeDtypeStruct((width, wide), BF16),
            jax.ShapeDtypeStruct((width, 2 * wide), BF16),
            jax.ShapeDtypeStruct((1, 3 * wide), F32),
            jax.ShapeDtypeStruct((head_devs * wide, width), BF16),
        ),
        in_specs=[smem()] + vmem(4),
        compiler_params=pltpu.CompilerParams(vmem_limit_bytes=56 * 1024 * 1024),
        name="prepare",
    )(
        head_at.reshape(1),
        qkv_weight,
        out_weight,
        query_bias.reshape(1, width),
        value_bias.reshape(1, width),
    )


def attend(query, blocks, heads, pieces):
    data, wide, _, total_at = lane_plan(heads)
    rows = query.shape[0]
    size = rows // pieces
    count = len(blocks)

    def kernel(*refs):
        query_ref, block_refs = refs[0], refs[1 : 1 + count]
        out_ref, logs_ref = refs[1 + count : 3 + count]
        piece_refs, acc_ref = refs[3 + count : -1], refs[-1]
        query = query_ref[...]
        for index, ref in enumerate(block_refs):
            key = ref[:, :wide]
            value = ref[:, wide:]
            for head in range(heads):
                _, mask = head_lanes(heads, head)
                scores = lax.dot_general(query * mask, key, NT, preferred_element_type=F32)
                weights = jnp.exp(scores).astype(BF16)
                part = jnp.dot(weights, value, preferred_element_type=F32)
                acc_ref[head] = part if index == 0 else acc_ref[head] + part
        out = jnp.zeros((rows, wide), F32)
        logs = []
        for head in range(heads):
            own, _ = head_lanes(heads, head)
            part = acc_ref[head]
            total = part[:, data : data + 1]
            out = out + (part / total) * own
            logs.append(jnp.log(total))
        out = out.astype(BF16)
        out_ref[...] = out
        for index, ref in enumerate(piece_refs):
            ref[...] = out[index * size : (index + 1) * size]
        logs_ref[...] = spread_parts(logs, total_at, wide).astype(BF16)

    shape = jax.ShapeDtypeStruct((rows, wide), BF16)
    small = jax.ShapeDtypeStruct((size, wide), BF16)
    return on_chip(
        kernel, (shape, shape) + (small,) * pieces, [pltpu.VMEM((heads, rows, wide), F32)]
    )(query, *blocks)


def project_back(grad, out_rows, pieces):
    rows = grad.shape[0]
    wide = out_rows.shape[0] // pieces

    def kernel(grad_ref, weight_ref, *outs):
        for index, ref in enumerate(outs):
            weight = weight_ref[index * wide : (index + 1) * wide]
            ref[...] = lax.dot_general(
                grad_ref[...], weight, NT, preferred_element_type=F32
            ).astype(BF16)

    return on_chip(kernel, (jax.ShapeDtypeStruct((rows, wide), BF16),) * pieces)(grad, out_rows)


def with_stats(blocks, attended, logs, heads):
    _, wide, delta_at, _ = lane_plan(heads)
    size = blocks[0].shape[0]
    count = len(blocks)

    def kernel(*refs):
        att_ref, logs_ref, out_ref = refs[count:]
        for index, ref in enumerate(refs[:count]):
            at = slice(index * size, (index + 1) * size)
            back = ref[...].astype(F32)
            prod = back * att_ref[at].astype(F32)
            deltas = []
            for head in range(heads):
                own, _ = head_lanes(heads, head)
                deltas.append(jnp.sum(prod * own, axis=-1, keepdims=True))
            out = back + spread_parts(deltas, delta_at, wide) + logs_ref[at].astype(F32)
            out_ref[at] = out.astype(BF16)

    return on_chip(kernel, jax.ShapeDtypeStruct(attended.shape, BF16))(*blocks, attended, logs)


def add_to(ref, head, index, part):
    ref[head] = part if index == 0 else ref[head] + part


def merge_heads(ref, factor):
    heads, rows, wide = ref.shape
    out = jnp.zeros((rows, wide), F32)
    for head in range(heads):
        own, _ = head_lanes(heads, head)
        out = out + ref[head] * (own * factor)
    return out.astype(BF16)


def total_lanes(heads):
    _, wide, _, total_at = lane_plan(heads)
    lane = lax.broadcasted_iota(jnp.int32, (1, wide), 1)
    return ((lane >= total_at) & (lane < total_at + 3 * heads)).astype(BF16)


def query_side(query, back, keyvals, heads):
    _, wide, _, _ = lane_plan(heads)
    rows = query.shape[0]

    def kernel(query_ref, back_ref, *refs):
        keyval_refs, (out_ref, acc_ref) = refs[:-2], refs[-2:]
        back_own = back_ref[...]
        query_own = query_ref[...] + back_own * total_lanes(heads)
        for index, ref in enumerate(keyval_refs):
            key, value = ref[:, :wide], ref[:, wide:]
            for head in range(heads):
                _, mask = head_lanes(heads, head)
                scores = lax.dot_general(query_own * mask, key, NT, preferred_element_type=F32)
                inner = lax.dot_general(back_own * mask, value, NT, preferred_element_type=F32)
                half = (jnp.exp(scores) * inner).astype(BF16)
                add_to(acc_ref, head, index, jnp.dot(half, key, preferred_element_type=F32))
        out_ref[...] = merge_heads(acc_ref, SCALE)

    return on_chip(
        kernel, jax.ShapeDtypeStruct((rows, wide), BF16), [pltpu.VMEM((heads, rows, wide), F32)]
    )(query, back, *keyvals)


def key_side(own, queries, backs, heads):
    _, wide, _, _ = lane_plan(heads)
    rows = queries[0].shape[0]
    count = len(queries)

    def kernel(*refs):
        own_refs, refs = refs[: len(own)], refs[len(own) :]
        query_refs, back_refs = refs[:count], refs[count : 2 * count]
        out_ref, dk_ref, dv_ref = refs[2 * count :]
        keyval = jnp.concatenate([ref[...] for ref in own_refs])
        key_own, value_own = keyval[:, :wide], keyval[:, wide:]
        for index in range(count):
            back_in = back_refs[index][...]
            query_plain = query_refs[index][...]
            query = query_plain + back_in * total_lanes(heads)
            for head in range(heads):
                _, mask = head_lanes(heads, head)
                scores = lax.dot_general(key_own * mask, query, NT, preferred_element_type=F32)
                probs = jnp.exp(scores)
                inner = lax.dot_general(value_own * mask, back_in, NT, preferred_element_type=F32)
                half = (probs * inner).astype(BF16)
                part = jnp.dot(probs.astype(BF16), back_in, preferred_element_type=F32)
                add_to(dv_ref, head, index, part)
                part = jnp.dot(half, query_plain, preferred_element_type=F32)
                add_to(dk_ref, head, index, part)
        out_ref[:, :wide] = merge_heads(dk_ref, 1.0)
        out_ref[:, wide:] = merge_heads(dv_ref, 1.0)

    acc = pltpu.VMEM((heads, rows, wide), F32)
    return on_chip(
        kernel, jax.ShapeDtypeStruct((rows, 2 * wide), BF16), [acc, acc]
    )(*own, *queries, *backs)


def weight_rows(grad_query, grad_keyval, rows, attended, grad_rows, core, heads):
    data, wide, _, _ = lane_plan(heads)
    width = rows.shape[1]
    total = 4 * data

    def kernel(core_ref, dq_ref, dkv_ref, rows_ref, att_ref, grad_rows_ref, keep_ref, send_ref, sums_ref, all_ref):
        rows_in = rows_ref[...]
        for slot in range(3):
            part = dq_ref[...] if slot == 0 else dkv_ref[:, (slot - 1) * wide : slot * wide]
            out = lax.dot_general(part, rows_in, TN, preferred_element_type=F32)
            all_ref[slot * data : (slot + 1) * data] = out[:data]
            sums_ref[slot : slot + 1] = jnp.sum(part.astype(F32), axis=0, keepdims=True)
        out = lax.dot_general(
            att_ref[...], grad_rows_ref[...], TN, preferred_element_type=F32
        )
        all_ref[3 * data :] = out[:data]
        half = total // 2
        mine = pl.multiple_of(core_ref[0] * half, 64)
        theirs = pl.multiple_of((1 - core_ref[0]) * half, 64)
        keep_ref[...] = all_ref[pl.ds(mine, half), :]
        send_ref[...] = all_ref[pl.ds(theirs, half), :].astype(BF16)

    return pl.pallas_call(
        kernel,
        out_shape=(
            jax.ShapeDtypeStruct((total // 2, width), F32),
            jax.ShapeDtypeStruct((total // 2, width), BF16),
            jax.ShapeDtypeStruct((3, wide), F32),
        ),
        in_specs=[smem()] + vmem(5),
        scratch_shapes=[pltpu.VMEM((total, width), F32)],
        compiler_params=pltpu.CompilerParams(vmem_limit_bytes=56 * 1024 * 1024),
        name="weight_rows",
    )(core.reshape(1), grad_query, grad_keyval, rows, attended, grad_rows)


def input_rows(grad_query, grad_keyval, q_own, kv_own, pieces):
    width = q_own.shape[0]
    size = grad_query.shape[0] // pieces

    def kernel(dq_ref, dkv_ref, q_ref, kv_ref, *outs):
        query = (dq_ref[...].astype(F32) * (1.0 / SCALE)).astype(BF16)
        out = lax.dot_general(query, q_ref[...], NT, preferred_element_type=F32)
        out = out + lax.dot_general(
            dkv_ref[...], kv_ref[...], NT, preferred_element_type=F32
        )
        out = out.astype(BF16)
        for index, ref in enumerate(outs):
            ref[...] = out[index * size : (index + 1) * size]

    return on_chip(
        kernel, (jax.ShapeDtypeStruct((size, width), BF16),) * pieces
    )(grad_query, grad_keyval, q_own, kv_own)


def assemble(arrays, bits, orders, head_at, head_devs, heads):
    data, _, _, _ = lane_plan(heads)
    width = head_devs * data
    total = 4 * data
    size = total >> len(bits)
    step = 256 if (3 * width) % 256 == 0 else 3 * width
    steps = 3 * width // step

    def kernel(at_ref, *refs):
        ins, (qkv_ref, out_ref, all_ref, turned_ref, sems) = refs[:8], refs[8:]
        own = [at_ref[index] for index in range(len(bits))]
        head = at_ref[len(bits)]
        for number, ref in enumerate(ins):
            side, partner, last = number // 4, number // 2 % 2, number % 2
            halving = orders[side]
            doubling = halving[::-1]
            lanes = slice(side * width // 2, (side + 1) * width // 2)
            for index in range(1 << (len(doubling) - 1)):
                flip = {place: (index >> at) & 1 for at, place in enumerate(doubling[:-1])}
                flip[doubling[-1]] = last
                start = (own[0] ^ partner) * (total // 2)
                for level, place in enumerate(halving):
                    start = start + (own[place] ^ flip[place]) * (total >> (level + 2))
                group = start // data
                within = start - group * data
                for hop_at in range(head_devs):
                    row = group * width + (head ^ hop_at) * data + within
                    from_row = (index * head_devs + hop_at) * size
                    all_ref[pl.ds(pl.multiple_of(row, 8), size), lanes] = ref[
                        from_row : from_row + size
                    ].astype(F32)
        copies = [pltpu.make_async_copy(all_ref.at[pl.ds(3 * width, width)], out_ref, sems.at[0])]
        copies[0].start()
        for index in range(steps):
            at = pl.ds(index * step, step)
            turned_ref[:, at] = all_ref[at].T
            copies.append(
                pltpu.make_async_copy(
                    turned_ref.at[:, at], qkv_ref.at[:, at], sems.at[index + 1]
                )
            )
            copies[-1].start()
        for copy in copies:
            copy.wait()

    return pl.pallas_call(
        kernel,
        out_shape=(
            jax.ShapeDtypeStruct((width, 3 * width), F32),
            jax.ShapeDtypeStruct((width, width), F32),
        ),
        in_specs=[smem()] + vmem(8),
        out_specs=(pl.BlockSpec(memory_space=pl.ANY),) * 2,
        scratch_shapes=[
            pltpu.VMEM((4 * width, width), F32),
            pltpu.VMEM((width, 3 * width), F32),
            pltpu.SemaphoreType.DMA((steps + 1,)),
        ],
        compiler_params=pltpu.CompilerParams(vmem_limit_bytes=56 * 1024 * 1024),
        name="assemble",
    )(jnp.stack(bits + [head_at]).astype(jnp.int32), *arrays)


def bits_of(axis):
    return [(axis, bit) for bit in range(lax.axis_size(axis).bit_length() - 1)]


def bit_value(place):
    axis, bit = place
    return (lax.axis_index(axis) >> bit) & 1


def hop(value, axis, distance):
    return lax.ppermute(value, axis, [(i, i ^ distance) for i in range(lax.axis_size(axis))])


def trade(value, place):
    return hop(value, place[0], 1 << place[1])


def after(value, *others):
    return lax.optimization_barrier((value, *others))[0]


def spread(value):
    high = lax.reduce_precision(value, 8, 7)
    return jnp.concatenate([high, value - high]).astype(BF16)


def halve_message(value, extra, place):
    half = value.shape[0] // 2
    mine = bit_value(place)
    send = lax.dynamic_slice_in_dim(value, (1 - mine) * half, half, 0).astype(BF16)
    keep = lax.dynamic_slice_in_dim(value, mine * half, half, 0)
    return jnp.concatenate([send, spread(extra)]), keep


def halve(value, extra, place):
    message, keep = halve_message(value, extra, place)
    return settle(keep, extra, trade(message, place))


def double(value, place):
    other = trade(value, place)
    first = bit_value(place) == 0
    return jnp.concatenate([jnp.where(first, value, other), jnp.where(first, other, value)])


def settle(keep, extra, got):
    half, count = keep.shape[0], extra.shape[0]
    got = got.astype(F32)
    return (
        keep + got[:half],
        extra + got[half : half + count] + got[half + count :],
    )


def scatter_weight(value):
    for place in bits_of("weight"):
        value = value.reshape((-1, 2) + value.shape[1:])
        mine = bit_value(place)
        send = lax.dynamic_index_in_dim(value, 1 - mine, 1, keepdims=False).astype(BF16)
        keep = lax.dynamic_index_in_dim(value, mine, 1, keepdims=False)
        value = keep + trade(send, place).astype(F32)
    return value[0]


def gather_blocks(value):
    blocks = [value]
    for place in bits_of("weight")[::-1] + bits_of("blk")[1:]:
        blocks = blocks + [trade(block, place) for block in blocks]
    return blocks


def gather_head(value):
    blocks = {0: value}
    for place in bits_of("head")[::-1]:
        blocks.update(
            {at | 1 << place[1]: trade(each, place) for at, each in blocks.items()}
        )
    return [blocks[at] for at in range(len(blocks))]


def per_device(
    hidden_in,
    qkv_weight,
    query_bias,
    value_bias,
    out_weight,
    out_bias,
    norm1_gain,
    norm1_bias,
    up_weight,
    up_bias,
    down_weight,
    down_bias,
    norm2_gain,
    norm2_bias,
    lengths,
    out_cotangent,
):
    rows_here, _, width = hidden_in.shape
    head_devs = lax.axis_size("head")
    weight_devs = lax.axis_size("weight")
    blk = lax.axis_index("blk")
    head_at = lax.axis_index("head")
    weight_at = lax.axis_index("weight")
    first_seq = (blk & 1) == 0
    heads = HEADS // head_devs
    data, wide, _, _ = lane_plan(heads)
    tokens = 2 * rows_here
    swap = ("blk", 0)

    def to_sequence(value):
        zero, one = value[:, 0], value[:, 1]
        mine = jnp.where(first_seq, zero, one)
        other = trade(jnp.where(first_seq, one, zero), swap)
        return jnp.concatenate([mine, other], axis=0)

    def from_sequence(value, narrow):
        mine = value[:rows_here]
        other = trade(value[rows_here:].astype(narrow), swap).astype(value.dtype)
        return jnp.stack(
            [jnp.where(first_seq, mine, other), jnp.where(first_seq, other, mine)], axis=1
        )

    flat = to_sequence(hidden_in)
    q_own, kv_own, bias_own, out_rows = prepare(
        after(qkv_weight, flat), out_weight, query_bias, value_bias, head_at, head_devs
    )
    hops = gather_head(flat)
    split = head_devs // 2
    near, far = jnp.concatenate(hops[:split]), jnp.concatenate(hops[split:])
    cotangent = to_sequence(after(out_cotangent, flat)).astype(F32)

    def project(part, first):
        index = jnp.arange(part.shape[0], dtype=jnp.int32)
        source = head_at ^ (first + index // tokens)
        within = index % tokens
        source_blk = blk ^ (within // rows_here)
        position = (
            (source_blk * head_devs + source) * weight_devs + weight_at
        ) * rows_here + within % rows_here
        valid = position < jnp.where(first_seq, lengths[0], lengths[1])
        lane = jnp.arange(2 * wide, dtype=jnp.int32)
        masked = jnp.where((lane == data)[None, :] & ~valid[:, None], FAR, 0.0)
        return (
            jnp.dot(part, kv_own, preferred_element_type=F32) + bias_own[:, wide:] + masked
        ).astype(BF16)

    own_keyvals = [project(near, 0), project(far, split)]
    keyvals = gather_blocks(own_keyvals[0])
    keyvals = keyvals + gather_blocks(own_keyvals[1])
    rows = jnp.concatenate([near, far])
    query = (
        jnp.dot(rows, q_own, preferred_element_type=F32) + bias_own[:, :wide]
    ).astype(BF16)
    attended, logs, *parts = attend(query, keyvals, heads, head_devs)
    queries = gather_blocks(after(query, attended))
    returned = [parts[0]] + [hop(parts[at], "head", at) for at in range(1, head_devs)]
    returned = jnp.concatenate(returned, axis=1)
    resid1 = flat.astype(F32) + jnp.dot(returned, out_rows, preferred_element_type=F32) + out_bias
    hidden1, normed1, rstd1 = norm_forward(resid1, norm1_gain, norm1_bias)
    gathered = lax.all_gather(hidden1.astype(BF16), "weight", axis=0, tiled=True)
    pre = jnp.dot(gathered, up_weight, preferred_element_type=F32) + up_bias
    active = gelu_value(pre).astype(BF16)
    mixed = scatter_weight(
        jnp.dot(active, down_weight, preferred_element_type=F32).reshape(
            weight_devs, tokens, width
        )
    )
    resid2 = hidden1 + mixed + down_bias
    final, normed2, rstd2 = norm_forward(resid2, norm2_gain, norm2_bias)
    grad_resid2, grad_norm2_gain, grad_norm2_bias = norm_backward(
        cotangent, normed2, rstd2, norm2_gain
    )
    grad_down_bias = jnp.sum(grad_resid2, axis=0)
    mixed_all = lax.all_gather(grad_resid2.astype(BF16), "weight", axis=0, tiled=True)
    grad_pre = lax.dot_general(
        mixed_all, down_weight, NT, preferred_element_type=F32
    ) * gelu_slope(pre)
    grad_up_bias = jnp.sum(grad_pre, axis=0)
    grad_pre_half = grad_pre.astype(BF16)
    back_hidden = scatter_weight(
        lax.dot_general(grad_pre_half, up_weight, NT, preferred_element_type=F32).reshape(
            weight_devs, tokens, width
        )
    )
    grad_down_weight = lax.dot_general(active, mixed_all, TN, preferred_element_type=F32)
    grad_up_weight = lax.dot_general(gathered, grad_pre_half, TN, preferred_element_type=F32)
    up_extra = jnp.pad(grad_up_bias[None], ((0, 7), (0, 0)))
    ffn_keep = jnp.where(first_seq, grad_up_weight, grad_down_weight)
    ffn_send = jnp.concatenate(
        [
            jnp.where(first_seq, grad_down_weight, grad_up_weight).astype(BF16),
            spread(up_extra),
        ]
    )
    grad_hidden1 = grad_resid2 + back_hidden
    grad_resid1, grad_norm1_gain, grad_norm1_bias = norm_backward(
        grad_hidden1, normed1, rstd1, norm1_gain
    )
    grad_out_bias = jnp.sum(grad_resid1, axis=0)
    grad_half, ffn_keep, ffn_send = lax.optimization_barrier(
        (grad_resid1.astype(BF16), ffn_keep, ffn_send)
    )
    ffn_got = trade(ffn_send, swap)
    ffn_places = bits_of("blk")[1:] + bits_of("head")
    layer_out = from_sequence(after(final.astype(BF16), grad_half), BF16)
    backs = project_back(grad_half, out_rows, head_devs)
    backs = [backs[0]] + [hop(backs[at], "head", at) for at in range(1, head_devs)]
    back = with_stats(backs, attended, logs, heads)
    back_blocks = gather_blocks(back)
    grad_late = after(grad_half, back)
    grad_rows = jnp.concatenate(
        [grad_late] + [hop(grad_late, "head", at) for at in range(1, head_devs)]
    )
    grad_query = query_side(query, back, keyvals, heads)
    ffn, up_extra = settle(ffn_keep, up_extra, after(ffn_got, grad_query))
    ffn_message, ffn_keep = halve_message(ffn, up_extra, ffn_places[0])
    ffn_got = trade(ffn_message, ffn_places[0])
    grad_keyval = key_side(own_keyvals, queries, back_blocks, heads)
    ffn, up_extra = settle(ffn_keep, up_extra, after(ffn_got, grad_keyval))
    for place in ffn_places[1:]:
        ffn, up_extra = halve(ffn, up_extra, place)
    ffn = ffn.astype(BF16)

    weight_bits, blk_bits = bits_of("weight"), bits_of("blk")
    core, middle, outer = weight_bits[0], weight_bits[1:], blk_bits
    keep, send, column_sums = weight_rows(
        grad_query, grad_keyval, rows, attended, grad_rows, bit_value(core), heads
    )
    column_sums = column_sums[:, :data]
    bias_rows = lax.dynamic_update_slice(
        jnp.zeros((2, head_devs, data), F32),
        jnp.stack([column_sums[0], column_sums[2]])[:, None],
        (0, head_at, 0),
    ).reshape(2, width)
    extra = jnp.concatenate(
        [
            bias_rows,
            jnp.stack([
                grad_out_bias,
                grad_norm1_gain,
                grad_norm1_bias,
                grad_norm2_gain,
                grad_norm2_bias,
                grad_down_bias,
            ]),
        ]
    )
    count = extra.shape[0]
    got = trade(jnp.concatenate([send, spread(extra)]), core)
    value, extra = settle(keep, extra, got)
    lane_half = width // 2
    orders = (middle + outer, outer + middle)
    sides = [
        (value[:, at * lane_half : (at + 1) * lane_half], extra[:, at * lane_half : (at + 1) * lane_half])
        for at in range(2)
    ]
    for level in range(len(middle + outer)):
        out = [halve_message(*sides[at], orders[at][level]) for at in range(2)]
        messages = lax.optimization_barrier((out[0][0], out[1][0]))
        got = [trade(messages[at], orders[at][level]) for at in range(2)]
        sides = [settle(out[at][1], sides[at][1], got[at]) for at in range(2)]
    sides = [jnp.concatenate([part.astype(BF16), spread(small)]) for part, small in sides]
    piece = jnp.concatenate(sides, axis=1)
    partial = input_rows(grad_query, grad_keyval, q_own, kv_own, head_devs)
    piece, *partial = lax.optimization_barrier((piece, *partial))
    pieces = gather_head(piece)
    size = piece.shape[0] - 2 * count
    small = sum(
        each[size : size + count].astype(F32) + each[size + count :].astype(F32)
        for each in pieces
    )
    stacked = jnp.concatenate([each[:size] for each in pieces])
    for place in ffn_places[:0:-1]:
        ffn = double(ffn, place)
    left, right = ffn[:, :lane_half], ffn[:, lane_half:]
    first_row = bit_value(ffn_places[0]) == 0

    def in_order(first, mine, other):
        return jnp.where(first, mine, other), jnp.where(first, other, mine)

    left_got, right_got = trade(left, ffn_places[0]), trade(right, swap)
    left = jnp.concatenate(in_order(first_row, left, left_got))
    right = jnp.concatenate(in_order(first_seq, right, right_got))
    left_got, right_got = trade(left, swap), trade(right, ffn_places[0])
    half_rows = right.shape[0] // 2
    up_left, down_left = in_order(first_seq, left, left_got)
    up_right = jnp.concatenate(in_order(first_row, right[:half_rows], right_got[:half_rows]))
    down_right = jnp.concatenate(in_order(first_row, right[half_rows:], right_got[half_rows:]))
    sides = [stacked[:, :lane_half], stacked[:, lane_half:]]
    count = len(middle + outer)
    for level in range(count - 1):
        got = [trade(sides[at], orders[at][::-1][level]) for at in range(2)]
        sides = [jnp.concatenate([sides[at], got[at]]) for at in range(2)]
    last = [trade(sides[at], orders[at][0]) for at in range(2)]
    arrays = [
        each
        for at in range(2)
        for each in (sides[at], last[at], trade(sides[at], core), trade(last[at], core))
    ]
    slot = {place: at for at, place in enumerate([core] + middle + outer)}
    grad_qkv_weight, grad_out_weight = assemble(
        arrays,
        [bit_value(place) for place in [core] + middle + outer],
        [[slot[at] for at in order] for order in orders],
        head_at,
        head_devs,
        heads,
    )

    partial = lax.optimization_barrier((*partial, stacked))[:-1]
    grad_in = grad_resid1 + partial[0].astype(F32)
    for at in range(1, head_devs):
        part = hop(partial[at], "head", at)
        grad_in = grad_in + part.astype(F32)
    grad_in = from_sequence(grad_in, BF16)
    return (
        layer_out,
        grad_in,
        grad_qkv_weight,
        small[0],
        small[1],
        grad_out_weight,
        small[2],
        small[3],
        small[4],
        jnp.concatenate([up_left, up_right], axis=1).astype(F32),
        up_extra[0],
        jnp.concatenate([down_left, down_right], axis=1).astype(F32),
        small[7],
        small[5],
        small[6],
    )


def solution(mesh):
    placed = (
        P(("blk", "head", "weight"), None, None),
        P(),
        P(),
        P(),
        P(),
        P(),
        P(),
        P(),
        P(None, "weight"),
        P("weight"),
        P("weight", None),
        P(),
        P(),
        P(),
        P(),
        P(("blk", "head", "weight"), None, None),
    )

    return jax.shard_map(
        per_device,
        mesh=mesh,
        in_specs=placed,
        out_specs=(
            P(("blk", "head", "weight"), None, None),
            P(("blk", "head", "weight"), None, None),
            P(),
            P(),
            P(),
            P(),
            P(),
            P(),
            P(),
            P(None, "weight"),
            P("weight"),
            P("weight", None),
            P(),
            P(),
            P(),
        ),
        check_vma=False,
    )
```

```python
import jax
import jax.numpy as jnp
from jax import lax
from jax.experimental import pallas as pl
from jax.experimental.pallas import tpu as pltpu
from jax.sharding import PartitionSpec as P


HEADS = 12
HEAD_DIM = 64
EPS = 1e-05
SQRT_HALF = 0.7071067811865476
INV_ROOT_TAU = 0.3989422804014327
SCALE = HEAD_DIM ** (-0.5)
FAR = -1e30
F32 = jnp.float32
BF16 = jnp.bfloat16
NT = (((1,), (1,)), ((), ()))
TN = (((0,), (0,)), ((), ()))


def norm_forward(resid, gain, bias):
    centre = jnp.mean(resid, axis=-1, keepdims=True)
    centred = resid - centre
    spread = jnp.mean(centred * centred, axis=-1, keepdims=True)
    rstd = lax.rsqrt(spread + EPS)
    normed = centred * rstd
    return (normed * gain + bias, normed, rstd)


def norm_backward(grad, normed, rstd, gain):
    scaled = grad * gain
    inner = (
        scaled
        - jnp.mean(scaled, axis=-1, keepdims=True)
        - normed * jnp.mean(scaled * normed, axis=-1, keepdims=True)
    )
    return (rstd * inner, jnp.sum(grad * normed, axis=0), jnp.sum(grad, axis=0))


def gelu_value(pre):
    return 0.5 * pre * (1.0 + lax.erf(pre * SQRT_HALF))


def gelu_slope(pre):
    return 0.5 * (1.0 + lax.erf(pre * SQRT_HALF)) + pre * jnp.exp(-0.5 * pre * pre) * INV_ROOT_TAU


def lane_plan(heads):
    data = heads * HEAD_DIM
    wide = -(-(data + 1 + 6 * heads) // 128) * 128
    return data, wide, data + 1, data + 1 + 3 * heads


def head_lanes(heads, head):
    data, wide, delta_at, total_at = lane_plan(heads)
    lane = lax.broadcasted_iota(jnp.int32, (1, wide), 1)

    def within(start, count):
        return (lane >= start) & (lane < start + count)

    own = within(head * HEAD_DIM, HEAD_DIM)
    extra = (
        (lane == data)
        | within(delta_at + 3 * head, 3)
        | within(total_at + 3 * head, 3)
    )
    return own.astype(F32), (own | extra).astype(BF16)


def three_parts(value):
    high = value.astype(BF16).astype(F32)
    rest = value - high
    middle = rest.astype(BF16).astype(F32)
    return high, middle, rest - middle


def spread_parts(value, start, wide):
    lane = lax.broadcasted_iota(jnp.int32, (1, wide), 1)
    out = 0.0
    for part, piece in enumerate(three_parts(value)):
        out = out + jnp.where(lane == start + part, piece, 0.0)
    return out


def on_chip(kernel, out_shape, scratch=()):
    return pl.pallas_call(
        kernel,
        out_shape=out_shape,
        scratch_shapes=list(scratch),
        compiler_params=pltpu.CompilerParams(vmem_limit_bytes=56 * 1024 * 1024),
    )


def smem():
    return pl.BlockSpec(memory_space=pltpu.SMEM)


def vmem(count):
    return [pl.BlockSpec(memory_space=pltpu.VMEM)] * count


def prepare(qkv_weight, out_weight, query_bias, value_bias, head_at, head_devs):
    heads = HEADS // head_devs
    data, wide, delta_at, total_at = lane_plan(heads)
    width = qkv_weight.shape[0]

    def kernel(at_ref, qkv_ref, out_ref, qb_ref, vb_ref, q_ref, kv_ref, bias_ref, rows_ref):
        at = at_ref[0]
        pair = at // 2
        odd = (at - 2 * pair).astype(F32)
        lane = lax.broadcasted_iota(jnp.int32, (1, wide), 1)
        keep = (lane < data).astype(F32)

        def pick(value):
            high = pltpu.roll(value, data, 1)
            return (value * (1.0 - odd) + high * odd)[:, :wide] * keep

        def columns(group):
            start = pl.multiple_of(group * width + pair * 2 * data, 128)
            return pick(qkv_ref[:, pl.ds(start, 2 * data)].astype(F32))

        q_ref[...] = (columns(0) * SCALE).astype(BF16)
        kv_ref[:, :wide] = columns(1).astype(BF16)
        kv_ref[:, wide:] = columns(2).astype(BF16)
        start = pl.ds(pl.multiple_of(pair * 2 * data, 128), 2 * data)
        ones = (lane == data).astype(F32)
        deltas = ((lane >= delta_at) & (lane < delta_at + 3 * heads)).astype(F32)
        totals = ((lane >= total_at) & (lane < total_at + 3 * heads)).astype(F32)
        query = pick(jnp.broadcast_to(qb_ref[:, start], (8, 2 * data)))[:1]
        value = pick(jnp.broadcast_to(vb_ref[:, start], (8, 2 * data)))[:1]
        bias_ref[:, :wide] = query * SCALE + ones
        bias_ref[:, wide : 2 * wide] = -totals
        bias_ref[:, 2 * wide :] = value + ones - deltas
        for hop in range(head_devs):
            source = pl.multiple_of((at ^ hop) * data, HEAD_DIM)
            rows_ref[hop * wide : hop * wide + data] = out_ref[pl.ds(source, data), :]
            rows_ref[hop * wide + data : (hop + 1) * wide] = jnp.zeros(
                (wide - data, width), BF16
            )

    return pl.pallas_call(
        kernel,
        out_shape=(
            jax.ShapeDtypeStruct((width, wide), BF16),
            jax.ShapeDtypeStruct((width, 2 * wide), BF16),
            jax.ShapeDtypeStruct((1, 3 * wide), F32),
            jax.ShapeDtypeStruct((head_devs * wide, width), BF16),
        ),
        in_specs=[smem()] + vmem(4),
        compiler_params=pltpu.CompilerParams(vmem_limit_bytes=56 * 1024 * 1024),
        name="prepare",
    )(
        head_at.reshape(1),
        qkv_weight,
        out_weight,
        query_bias.reshape(1, width),
        value_bias.reshape(1, width),
    )


def attend(query, blocks, heads, pieces):
    data, wide, _, total_at = lane_plan(heads)
    rows = query.shape[0]
    size = rows // pieces
    count = len(blocks)

    def kernel(*refs):
        query_ref, block_refs = refs[0], refs[1 : 1 + count]
        out_ref, logs_ref = refs[1 + count : 3 + count]
        piece_refs, acc_ref = refs[3 + count : -1], refs[-1]
        acc_ref[...] = jnp.zeros_like(acc_ref)

        def one_head(head):
            own, mask = head_lanes(heads, head)
            query = query_ref[...] * mask
            acc = 0.0
            for ref in block_refs:
                scores = lax.dot_general(query, ref[:, :wide], NT, preferred_element_type=F32)
                weights = jnp.exp(scores).astype(BF16)
                acc = acc + jnp.dot(weights, ref[:, wide:], preferred_element_type=F32)
            total = acc[:, data : data + 1]
            acc_ref[0] += (acc / total) * own
            acc_ref[1] += spread_parts(jnp.log(total), total_at + 3 * head, wide)

        for head in range(heads):
            one_head(head)
        out = acc_ref[0].astype(BF16)
        out_ref[...] = out
        for index, ref in enumerate(piece_refs):
            ref[...] = out[index * size : (index + 1) * size]
        logs_ref[...] = acc_ref[1].astype(BF16)

    shape = jax.ShapeDtypeStruct((rows, wide), BF16)
    small = jax.ShapeDtypeStruct((size, wide), BF16)
    return on_chip(
        kernel, (shape, shape) + (small,) * pieces, [pltpu.VMEM((2, rows, wide), F32)]
    )(query, *blocks)


def project_back(grad, out_rows, pieces):
    rows = grad.shape[0]
    wide = out_rows.shape[0] // pieces

    def kernel(grad_ref, weight_ref, *outs):
        for index, ref in enumerate(outs):
            weight = weight_ref[index * wide : (index + 1) * wide]
            ref[...] = lax.dot_general(
                grad_ref[...], weight, NT, preferred_element_type=F32
            ).astype(BF16)

    return on_chip(kernel, (jax.ShapeDtypeStruct((rows, wide), BF16),) * pieces)(grad, out_rows)


def with_stats(blocks, attended, logs, heads):
    _, wide, delta_at, _ = lane_plan(heads)
    size = blocks[0].shape[0]
    count = len(blocks)

    def kernel(*refs):
        att_ref, logs_ref, out_ref = refs[count:]
        for index, ref in enumerate(refs[:count]):
            at = slice(index * size, (index + 1) * size)
            back = ref[...].astype(F32)
            prod = back * att_ref[at].astype(F32)
            out = back + logs_ref[at].astype(F32)
            for head in range(heads):
                own, _ = head_lanes(heads, head)
                delta = jnp.sum(prod * own, axis=-1, keepdims=True)
                out = out + spread_parts(delta, delta_at + 3 * head, wide)
            out_ref[at] = out.astype(BF16)

    return on_chip(kernel, jax.ShapeDtypeStruct(attended.shape, BF16))(*blocks, attended, logs)


def total_lanes(heads):
    _, wide, _, total_at = lane_plan(heads)
    lane = lax.broadcasted_iota(jnp.int32, (1, wide), 1)
    return ((lane >= total_at) & (lane < total_at + 3 * heads)).astype(BF16)


def query_side(query, back, keyvals, heads):
    _, wide, _, _ = lane_plan(heads)
    rows = query.shape[0]

    def kernel(query_ref, back_ref, *refs):
        keyval_refs, (out_ref, acc_ref) = refs[:-2], refs[-2:]
        acc_ref[...] = jnp.zeros_like(acc_ref)

        def one_head(head, _):
            own, mask = head_lanes(heads, head)
            back_own = back_ref[...] * mask
            query_own = query_ref[...] * mask + back_own * total_lanes(heads)
            acc = 0.0
            for ref in keyval_refs:
                key = ref[:, :wide]
                scores = lax.dot_general(query_own, key, NT, preferred_element_type=F32)
                inner = lax.dot_general(back_own, ref[:, wide:], NT, preferred_element_type=F32)
                half = (jnp.exp(scores) * inner).astype(BF16)
                acc = acc + jnp.dot(half, key, preferred_element_type=F32)
            acc_ref[...] += acc * (own * SCALE)
            return 0

        lax.fori_loop(0, heads, one_head, 0)
        out_ref[...] = acc_ref[...].astype(BF16)

    return on_chip(
        kernel, jax.ShapeDtypeStruct((rows, wide), BF16), [pltpu.VMEM((rows, wide), F32)]
    )(query, back, *keyvals)


def key_side(own, queries, backs, heads):
    _, wide, _, _ = lane_plan(heads)
    rows = queries[0].shape[0]
    count = len(queries)

    def kernel(*refs):
        own_refs, refs = refs[: len(own)], refs[len(own) :]
        query_refs, back_refs = refs[:count], refs[count : 2 * count]
        out_ref, dk_ref, dv_ref = refs[2 * count :]
        keyval = jnp.concatenate([ref[...] for ref in own_refs])
        dk_ref[...] = jnp.zeros_like(dk_ref)
        dv_ref[...] = jnp.zeros_like(dv_ref)

        def one_head(head, _):
            own_lanes, mask = head_lanes(heads, head)
            key_own, value_own = keyval[:, :wide] * mask, keyval[:, wide:] * mask
            dk = dv = 0.0
            for query_ref, back_ref in zip(query_refs, back_refs):
                back_in = back_ref[...]
                query_plain = query_ref[...]
                query = query_plain + back_in * total_lanes(heads)
                scores = lax.dot_general(key_own, query, NT, preferred_element_type=F32)
                probs = jnp.exp(scores)
                inner = lax.dot_general(value_own, back_in, NT, preferred_element_type=F32)
                half = (probs * inner).astype(BF16)
                dv = dv + jnp.dot(probs.astype(BF16), back_in, preferred_element_type=F32)
                dk = dk + jnp.dot(half, query_plain, preferred_element_type=F32)
            dk_ref[...] += dk * own_lanes
            dv_ref[...] += dv * own_lanes
            return 0

        lax.fori_loop(0, heads, one_head, 0)
        out_ref[:, :wide] = dk_ref[...].astype(BF16)
        out_ref[:, wide:] = dv_ref[...].astype(BF16)

    acc = pltpu.VMEM((rows, wide), F32)
    return on_chip(
        kernel, jax.ShapeDtypeStruct((rows, 2 * wide), BF16), [acc, acc]
    )(*own, *queries, *backs)


def weight_rows(grad_query, grad_keyval, rows, attended, grad_rows, core, heads):
    data, wide, _, _ = lane_plan(heads)
    width = rows.shape[1]
    total = 4 * data

    def kernel(core_ref, dq_ref, dkv_ref, rows_ref, att_ref, grad_rows_ref, keep_ref, send_ref, sums_ref, all_ref):
        rows_in = rows_ref[...]
        for slot in range(3):
            part = dq_ref[...] if slot == 0 else dkv_ref[:, (slot - 1) * wide : slot * wide]
            out = lax.dot_general(part, rows_in, TN, preferred_element_type=F32)
            all_ref[slot * data : (slot + 1) * data] = out[:data]
            sums_ref[slot : slot + 1] = jnp.sum(part.astype(F32), axis=0, keepdims=True)
        out = lax.dot_general(
            att_ref[...], grad_rows_ref[...], TN, preferred_element_type=F32
        )
        all_ref[3 * data :] = out[:data]
        half = total // 2
        mine = pl.multiple_of(core_ref[0] * half, 64)
        theirs = pl.multiple_of((1 - core_ref[0]) * half, 64)
        keep_ref[...] = all_ref[pl.ds(mine, half), :]
        send_ref[...] = all_ref[pl.ds(theirs, half), :].astype(BF16)

    return pl.pallas_call(
        kernel,
        out_shape=(
            jax.ShapeDtypeStruct((total // 2, width), F32),
            jax.ShapeDtypeStruct((total // 2, width), BF16),
            jax.ShapeDtypeStruct((3, wide), F32),
        ),
        in_specs=[smem()] + vmem(5),
        scratch_shapes=[pltpu.VMEM((total, width), F32)],
        compiler_params=pltpu.CompilerParams(vmem_limit_bytes=56 * 1024 * 1024),
        name="weight_rows",
    )(core.reshape(1), grad_query, grad_keyval, rows, attended, grad_rows)


def input_rows(grad_query, grad_keyval, q_own, kv_own, pieces):
    width = q_own.shape[0]
    size = grad_query.shape[0] // pieces

    def kernel(dq_ref, dkv_ref, q_ref, kv_ref, *outs):
        query = (dq_ref[...].astype(F32) * (1.0 / SCALE)).astype(BF16)
        out = lax.dot_general(query, q_ref[...], NT, preferred_element_type=F32)
        out = out + lax.dot_general(
            dkv_ref[...], kv_ref[...], NT, preferred_element_type=F32
        )
        out = out.astype(BF16)
        for index, ref in enumerate(outs):
            ref[...] = out[index * size : (index + 1) * size]

    return on_chip(
        kernel, (jax.ShapeDtypeStruct((size, width), BF16),) * pieces
    )(grad_query, grad_keyval, q_own, kv_own)


def assemble(arrays, bits, orders, head_at, head_devs, heads):
    data, _, _, _ = lane_plan(heads)
    width = head_devs * data
    total = 4 * data
    size = total >> len(bits)
    step = 256 if (3 * width) % 256 == 0 else 3 * width
    steps = 3 * width // step

    def kernel(at_ref, *refs):
        ins, (qkv_ref, out_ref, all_ref, turned_ref, sems) = refs[:8], refs[8:]
        own = [at_ref[index] for index in range(len(bits))]
        head = at_ref[len(bits)]
        for number, ref in enumerate(ins):
            side, partner, last = number // 4, number // 2 % 2, number % 2
            halving = orders[side]
            doubling = halving[::-1]
            lanes = slice(side * width // 2, (side + 1) * width // 2)
            for index in range(1 << (len(doubling) - 1)):
                flip = {place: (index >> at) & 1 for at, place in enumerate(doubling[:-1])}
                flip[doubling[-1]] = last
                start = (own[0] ^ partner) * (total // 2)
                for level, place in enumerate(halving):
                    start = start + (own[place] ^ flip[place]) * (total >> (level + 2))
                group = start // data
                within = start - group * data
                for hop_at in range(head_devs):
                    row = group * width + (head ^ hop_at) * data + within
                    from_row = (index * head_devs + hop_at) * size
                    all_ref[pl.ds(pl.multiple_of(row, 8), size), lanes] = ref[
                        from_row : from_row + size
                    ].astype(F32)
        copies = [pltpu.make_async_copy(all_ref.at[pl.ds(3 * width, width)], out_ref, sems.at[0])]
        copies[0].start()
        for index in range(steps):
            at = pl.ds(index * step, step)
            turned_ref[:, at] = all_ref[at].T
            copies.append(
                pltpu.make_async_copy(
                    turned_ref.at[:, at], qkv_ref.at[:, at], sems.at[index + 1]
                )
            )
            copies[-1].start()
        for copy in copies:
            copy.wait()

    return pl.pallas_call(
        kernel,
        out_shape=(
            jax.ShapeDtypeStruct((width, 3 * width), F32),
            jax.ShapeDtypeStruct((width, width), F32),
        ),
        in_specs=[smem()] + vmem(8),
        out_specs=(pl.BlockSpec(memory_space=pl.ANY),) * 2,
        scratch_shapes=[
            pltpu.VMEM((4 * width, width), F32),
            pltpu.VMEM((width, 3 * width), F32),
            pltpu.SemaphoreType.DMA((steps + 1,)),
        ],
        compiler_params=pltpu.CompilerParams(vmem_limit_bytes=56 * 1024 * 1024),
        name="assemble",
    )(jnp.stack(bits + [head_at]).astype(jnp.int32), *arrays)


def bits_of(axis):
    return [(axis, bit) for bit in range(lax.axis_size(axis).bit_length() - 1)]


def bit_value(place):
    axis, bit = place
    return (lax.axis_index(axis) >> bit) & 1


def hop(value, axis, distance):
    return lax.ppermute(value, axis, [(i, i ^ distance) for i in range(lax.axis_size(axis))])


def trade(value, place):
    return hop(value, place[0], 1 << place[1])


def after(value, *others):
    return lax.optimization_barrier((value, *others))[0]


def spread(value):
    high = lax.reduce_precision(value, 8, 7)
    return jnp.concatenate([high, value - high]).astype(BF16)


def halve_message(value, extra, place):
    half = value.shape[0] // 2
    mine = bit_value(place)
    send = lax.dynamic_slice_in_dim(value, (1 - mine) * half, half, 0).astype(BF16)
    keep = lax.dynamic_slice_in_dim(value, mine * half, half, 0)
    return jnp.concatenate([send, spread(extra)]), keep


def halve(value, extra, place):
    message, keep = halve_message(value, extra, place)
    return settle(keep, extra, trade(message, place))


def double(value, place):
    other = trade(value, place)
    first = bit_value(place) == 0
    return jnp.concatenate([jnp.where(first, value, other), jnp.where(first, other, value)])


def settle(keep, extra, got):
    half, count = keep.shape[0], extra.shape[0]
    got = got.astype(F32)
    return (
        keep + got[:half],
        extra + got[half : half + count] + got[half + count :],
    )


def scatter_weight(value):
    for place in bits_of("weight"):
        value = value.reshape((-1, 2) + value.shape[1:])
        mine = bit_value(place)
        send = lax.dynamic_index_in_dim(value, 1 - mine, 1, keepdims=False).astype(BF16)
        keep = lax.dynamic_index_in_dim(value, mine, 1, keepdims=False)
        value = keep + trade(send, place).astype(F32)
    return value[0]


def gather_blocks(value):
    blocks = [value]
    for place in bits_of("weight")[::-1] + bits_of("blk")[1:]:
        blocks = blocks + [trade(block, place) for block in blocks]
    return blocks


def gather_head(value):
    blocks = {0: value}
    for place in bits_of("head")[::-1]:
        blocks.update(
            {at | 1 << place[1]: trade(each, place) for at, each in blocks.items()}
        )
    return [blocks[at] for at in range(len(blocks))]


def per_device(
    hidden_in,
    qkv_weight,
    query_bias,
    value_bias,
    out_weight,
    out_bias,
    norm1_gain,
    norm1_bias,
    up_weight,
    up_bias,
    down_weight,
    down_bias,
    norm2_gain,
    norm2_bias,
    lengths,
    out_cotangent,
):
    rows_here, _, width = hidden_in.shape
    head_devs = lax.axis_size("head")
    weight_devs = lax.axis_size("weight")
    blk = lax.axis_index("blk")
    head_at = lax.axis_index("head")
    weight_at = lax.axis_index("weight")
    first_seq = (blk & 1) == 0
    heads = HEADS // head_devs
    data, wide, _, _ = lane_plan(heads)
    tokens = 2 * rows_here
    swap = ("blk", 0)

    def to_sequence(value):
        zero, one = value[:, 0], value[:, 1]
        mine = jnp.where(first_seq, zero, one)
        other = trade(jnp.where(first_seq, one, zero), swap)
        return jnp.concatenate([mine, other], axis=0)

    def from_sequence(value, narrow):
        mine = value[:rows_here]
        other = trade(value[rows_here:].astype(narrow), swap).astype(value.dtype)
        return jnp.stack(
            [jnp.where(first_seq, mine, other), jnp.where(first_seq, other, mine)], axis=1
        )

    flat = to_sequence(hidden_in)
    q_own, kv_own, bias_own, out_rows = prepare(
        after(qkv_weight, flat), out_weight, query_bias, value_bias, head_at, head_devs
    )
    hops = gather_head(flat)
    split = head_devs // 2
    near, far = jnp.concatenate(hops[:split]), jnp.concatenate(hops[split:])
    cotangent = to_sequence(after(out_cotangent, flat)).astype(F32)

    def project(part, first):
        index = jnp.arange(part.shape[0], dtype=jnp.int32)
        source = head_at ^ (first + index // tokens)
        within = index % tokens
        source_blk = blk ^ (within // rows_here)
        position = (
            (source_blk * head_devs + source) * weight_devs + weight_at
        ) * rows_here + within % rows_here
        valid = position < jnp.where(first_seq, lengths[0], lengths[1])
        lane = jnp.arange(2 * wide, dtype=jnp.int32)
        masked = jnp.where((lane == data)[None, :] & ~valid[:, None], FAR, 0.0)
        return (
            jnp.dot(part, kv_own, preferred_element_type=F32) + bias_own[:, wide:] + masked
        ).astype(BF16)

    own_keyvals = [project(near, 0), project(far, split)]
    keyvals = gather_blocks(own_keyvals[0])
    keyvals = keyvals + gather_blocks(own_keyvals[1])
    rows = jnp.concatenate([near, far])
    query = (
        jnp.dot(rows, q_own, preferred_element_type=F32) + bias_own[:, :wide]
    ).astype(BF16)
    attended, logs, *parts = attend(query, keyvals, heads, head_devs)
    queries = gather_blocks(after(query, attended))
    returned = [parts[0]] + [hop(parts[at], "head", at) for at in range(1, head_devs)]
    returned = jnp.concatenate(returned, axis=1)
    resid1 = flat.astype(F32) + jnp.dot(returned, out_rows, preferred_element_type=F32) + out_bias
    hidden1, normed1, rstd1 = norm_forward(resid1, norm1_gain, norm1_bias)
    gathered = lax.all_gather(hidden1.astype(BF16), "weight", axis=0, tiled=True)
    pre = jnp.dot(gathered, up_weight, preferred_element_type=F32) + up_bias
    active = gelu_value(pre).astype(BF16)
    mixed = scatter_weight(
        jnp.dot(active, down_weight, preferred_element_type=F32).reshape(
            weight_devs, tokens, width
        )
    )
    resid2 = hidden1 + mixed + down_bias
    final, normed2, rstd2 = norm_forward(resid2, norm2_gain, norm2_bias)
    grad_resid2, grad_norm2_gain, grad_norm2_bias = norm_backward(
        cotangent, normed2, rstd2, norm2_gain
    )
    grad_down_bias = jnp.sum(grad_resid2, axis=0)
    mixed_all = lax.all_gather(grad_resid2.astype(BF16), "weight", axis=0, tiled=True)
    grad_pre = lax.dot_general(
        mixed_all, down_weight, NT, preferred_element_type=F32
    ) * gelu_slope(pre)
    grad_up_bias = jnp.sum(grad_pre, axis=0)
    grad_pre_half = grad_pre.astype(BF16)
    back_hidden = scatter_weight(
        lax.dot_general(grad_pre_half, up_weight, NT, preferred_element_type=F32).reshape(
            weight_devs, tokens, width
        )
    )
    grad_down_weight = lax.dot_general(active, mixed_all, TN, preferred_element_type=F32)
    grad_up_weight = lax.dot_general(gathered, grad_pre_half, TN, preferred_element_type=F32)
    up_extra = jnp.pad(grad_up_bias[None], ((0, 7), (0, 0)))
    ffn_keep = jnp.where(first_seq, grad_up_weight, grad_down_weight)
    ffn_send = jnp.concatenate(
        [
            jnp.where(first_seq, grad_down_weight, grad_up_weight).astype(BF16),
            spread(up_extra),
        ]
    )
    grad_hidden1 = grad_resid2 + back_hidden
    grad_resid1, grad_norm1_gain, grad_norm1_bias = norm_backward(
        grad_hidden1, normed1, rstd1, norm1_gain
    )
    grad_out_bias = jnp.sum(grad_resid1, axis=0)
    grad_half, ffn_keep, ffn_send = lax.optimization_barrier(
        (grad_resid1.astype(BF16), ffn_keep, ffn_send)
    )
    ffn_got = trade(ffn_send, swap)
    ffn_places = bits_of("blk")[1:] + bits_of("head")
    layer_out = from_sequence(after(final.astype(BF16), grad_half), BF16)
    backs = project_back(grad_half, out_rows, head_devs)
    backs = [backs[0]] + [hop(backs[at], "head", at) for at in range(1, head_devs)]
    back = with_stats(backs, attended, logs, heads)
    back_blocks = gather_blocks(back)
    grad_late = after(grad_half, back)
    grad_rows = jnp.concatenate(
        [grad_late] + [hop(grad_late, "head", at) for at in range(1, head_devs)]
    )
    grad_query = query_side(query, back, keyvals, heads)
    ffn, up_extra = settle(ffn_keep, up_extra, after(ffn_got, grad_query))
    ffn_message, ffn_keep = halve_message(ffn, up_extra, ffn_places[0])
    ffn_got = trade(ffn_message, ffn_places[0])
    grad_keyval = key_side(own_keyvals, queries, back_blocks, heads)
    ffn, up_extra = settle(ffn_keep, up_extra, after(ffn_got, grad_keyval))
    for place in ffn_places[1:]:
        ffn, up_extra = halve(ffn, up_extra, place)
    ffn = ffn.astype(BF16)

    weight_bits, blk_bits = bits_of("weight"), bits_of("blk")
    core, middle, outer = weight_bits[0], weight_bits[1:], blk_bits
    keep, send, column_sums = weight_rows(
        grad_query, grad_keyval, rows, attended, grad_rows, bit_value(core), heads
    )
    column_sums = column_sums[:, :data]
    bias_rows = lax.dynamic_update_slice(
        jnp.zeros((2, head_devs, data), F32),
        jnp.stack([column_sums[0], column_sums[2]])[:, None],
        (0, head_at, 0),
    ).reshape(2, width)
    extra = jnp.concatenate(
        [
            bias_rows,
            jnp.stack([
                grad_out_bias,
                grad_norm1_gain,
                grad_norm1_bias,
                grad_norm2_gain,
                grad_norm2_bias,
                grad_down_bias,
            ]),
        ]
    )
    count = extra.shape[0]
    got = trade(jnp.concatenate([send, spread(extra)]), core)
    value, extra = settle(keep, extra, got)
    lane_half = width // 2
    orders = (middle + outer, outer + middle)
    sides = [
        (value[:, at * lane_half : (at + 1) * lane_half], extra[:, at * lane_half : (at + 1) * lane_half])
        for at in range(2)
    ]
    for level in range(len(middle + outer)):
        out = [halve_message(*sides[at], orders[at][level]) for at in range(2)]
        messages = lax.optimization_barrier((out[0][0], out[1][0]))
        got = [trade(messages[at], orders[at][level]) for at in range(2)]
        sides = [settle(out[at][1], sides[at][1], got[at]) for at in range(2)]
    sides = [jnp.concatenate([part.astype(BF16), spread(small)]) for part, small in sides]
    piece = jnp.concatenate(sides, axis=1)
    partial = input_rows(grad_query, grad_keyval, q_own, kv_own, head_devs)
    piece, *partial = lax.optimization_barrier((piece, *partial))
    pieces = gather_head(piece)
    size = piece.shape[0] - 2 * count
    small = sum(
        each[size : size + count].astype(F32) + each[size + count :].astype(F32)
        for each in pieces
    )
    stacked = jnp.concatenate([each[:size] for each in pieces])
    for place in ffn_places[:0:-1]:
        ffn = double(ffn, place)
    left, right = ffn[:, :lane_half], ffn[:, lane_half:]
    first_row = bit_value(ffn_places[0]) == 0

    def in_order(first, mine, other):
        return jnp.where(first, mine, other), jnp.where(first, other, mine)

    left_got, right_got = trade(left, ffn_places[0]), trade(right, swap)
    left = jnp.concatenate(in_order(first_row, left, left_got))
    right = jnp.concatenate(in_order(first_seq, right, right_got))
    left_got, right_got = trade(left, swap), trade(right, ffn_places[0])
    half_rows = right.shape[0] // 2
    up_left, down_left = in_order(first_seq, left, left_got)
    up_right = jnp.concatenate(in_order(first_row, right[:half_rows], right_got[:half_rows]))
    down_right = jnp.concatenate(in_order(first_row, right[half_rows:], right_got[half_rows:]))
    sides = [stacked[:, :lane_half], stacked[:, lane_half:]]
    count = len(middle + outer)
    for level in range(count - 1):
        got = [trade(sides[at], orders[at][::-1][level]) for at in range(2)]
        sides = [jnp.concatenate([sides[at], got[at]]) for at in range(2)]
    last = [trade(sides[at], orders[at][0]) for at in range(2)]
    arrays = [
        each
        for at in range(2)
        for each in (sides[at], last[at], trade(sides[at], core), trade(last[at], core))
    ]
    slot = {place: at for at, place in enumerate([core] + middle + outer)}
    grad_qkv_weight, grad_out_weight = assemble(
        arrays,
        [bit_value(place) for place in [core] + middle + outer],
        [[slot[at] for at in order] for order in orders],
        head_at,
        head_devs,
        heads,
    )

    partial = lax.optimization_barrier((*partial, stacked))[:-1]
    grad_in = grad_resid1 + partial[0].astype(F32)
    for at in range(1, head_devs):
        part = hop(partial[at], "head", at)
        grad_in = grad_in + part.astype(F32)
    grad_in = from_sequence(grad_in, BF16)
    return (
        layer_out,
        grad_in,
        grad_qkv_weight,
        small[0],
        small[1],
        grad_out_weight,
        small[2],
        small[3],
        small[4],
        jnp.concatenate([up_left, up_right], axis=1).astype(F32),
        up_extra[0],
        jnp.concatenate([down_left, down_right], axis=1).astype(F32),
        small[7],
        small[5],
        small[6],
    )


def solution(mesh):
    placed = (
        P(("blk", "head", "weight"), None, None),
        P(),
        P(),
        P(),
        P(),
        P(),
        P(),
        P(),
        P(None, "weight"),
        P("weight"),
        P("weight", None),
        P(),
        P(),
        P(),
        P(),
        P(("blk", "head", "weight"), None, None),
    )

    return jax.shard_map(
        per_device,
        mesh=mesh,
        in_specs=placed,
        out_specs=(
            P(("blk", "head", "weight"), None, None),
            P(("blk", "head", "weight"), None, None),
            P(),
            P(),
            P(),
            P(),
            P(),
            P(),
            P(),
            P(None, "weight"),
            P("weight"),
            P("weight", None),
            P(),
            P(),
            P(),
        ),
        check_vma=False,
    )
```

```python
import jax
import jax.numpy as jnp
from jax import lax
from jax.experimental import pallas as pl
from jax.experimental.pallas import tpu as pltpu
from jax.sharding import PartitionSpec as P


HEADS = 12
HEAD_DIM = 64
EPS = 1e-05
SQRT_HALF = 0.7071067811865476
INV_ROOT_TAU = 0.3989422804014327
SCALE = HEAD_DIM ** (-0.5)
FAR = -1e30
F32 = jnp.float32
BF16 = jnp.bfloat16
NT = (((1,), (1,)), ((), ()))
TN = (((0,), (0,)), ((), ()))


def norm_forward(resid, gain, bias):
    centre = jnp.mean(resid, axis=-1, keepdims=True)
    centred = resid - centre
    spread = jnp.mean(centred * centred, axis=-1, keepdims=True)
    rstd = lax.rsqrt(spread + EPS)
    normed = centred * rstd
    return (normed * gain + bias, normed, rstd)


def norm_backward(grad, normed, rstd, gain):
    scaled = grad * gain
    inner = (
        scaled
        - jnp.mean(scaled, axis=-1, keepdims=True)
        - normed * jnp.mean(scaled * normed, axis=-1, keepdims=True)
    )
    return (rstd * inner, jnp.sum(grad * normed, axis=0), jnp.sum(grad, axis=0))


def gelu_value(pre):
    return 0.5 * pre * (1.0 + lax.erf(pre * SQRT_HALF))


def gelu_slope(pre):
    return 0.5 * (1.0 + lax.erf(pre * SQRT_HALF)) + pre * jnp.exp(-0.5 * pre * pre) * INV_ROOT_TAU


def lane_plan(heads):
    data = heads * HEAD_DIM
    wide = -(-(data + 1 + 6 * heads) // 128) * 128
    return data, wide, data + 1, data + 1 + 3 * heads


def head_lanes(heads, head):
    data, wide, delta_at, total_at = lane_plan(heads)
    lane = lax.broadcasted_iota(jnp.int32, (1, wide), 1)

    def within(start, count):
        return (lane >= start) & (lane < start + count)

    own = within(head * HEAD_DIM, HEAD_DIM)
    extra = (
        (lane == data)
        | within(delta_at + 3 * head, 3)
        | within(total_at + 3 * head, 3)
    )
    return own.astype(F32), (own | extra).astype(BF16)


def three_parts(value):
    high = value.astype(BF16).astype(F32)
    rest = value - high
    middle = rest.astype(BF16).astype(F32)
    return high, middle, rest - middle


def spread_parts(value, start, wide):
    lane = lax.broadcasted_iota(jnp.int32, (1, wide), 1)
    out = 0.0
    for part, piece in enumerate(three_parts(value)):
        out = out + jnp.where(lane == start + part, piece, 0.0)
    return out


def on_chip(kernel, out_shape, scratch=()):
    return pl.pallas_call(
        kernel,
        out_shape=out_shape,
        scratch_shapes=list(scratch),
        compiler_params=pltpu.CompilerParams(vmem_limit_bytes=56 * 1024 * 1024),
    )


def smem():
    return pl.BlockSpec(memory_space=pltpu.SMEM)


def vmem(count):
    return [pl.BlockSpec(memory_space=pltpu.VMEM)] * count


def prepare(qkv_weight, out_weight, query_bias, value_bias, head_at, head_devs):
    heads = HEADS // head_devs
    data, wide, delta_at, total_at = lane_plan(heads)
    width = qkv_weight.shape[0]

    def kernel(at_ref, qkv_ref, out_ref, qb_ref, vb_ref, q_ref, kv_ref, bias_ref, rows_ref):
        at = at_ref[0]
        pair = at // 2
        odd = (at - 2 * pair).astype(F32)
        lane = lax.broadcasted_iota(jnp.int32, (1, wide), 1)
        keep = (lane < data).astype(F32)

        def pick(value):
            high = pltpu.roll(value, data, 1)
            return (value * (1.0 - odd) + high * odd)[:, :wide] * keep

        def columns(group):
            start = pl.multiple_of(group * width + pair * 2 * data, 128)
            return pick(qkv_ref[:, pl.ds(start, 2 * data)].astype(F32))

        q_ref[...] = (columns(0) * SCALE).astype(BF16)
        kv_ref[:, :wide] = columns(1).astype(BF16)
        kv_ref[:, wide:] = columns(2).astype(BF16)
        start = pl.ds(pl.multiple_of(pair * 2 * data, 128), 2 * data)
        ones = (lane == data).astype(F32)
        deltas = ((lane >= delta_at) & (lane < delta_at + 3 * heads)).astype(F32)
        totals = ((lane >= total_at) & (lane < total_at + 3 * heads)).astype(F32)
        query = pick(jnp.broadcast_to(qb_ref[:, start], (8, 2 * data)))[:1]
        value = pick(jnp.broadcast_to(vb_ref[:, start], (8, 2 * data)))[:1]
        bias_ref[:, :wide] = query * SCALE + ones
        bias_ref[:, wide : 2 * wide] = -totals
        bias_ref[:, 2 * wide :] = value + ones - deltas
        for hop in range(head_devs):
            source = pl.multiple_of((at ^ hop) * data, HEAD_DIM)
            rows_ref[hop * wide : hop * wide + data] = out_ref[pl.ds(source, data), :]
            rows_ref[hop * wide + data : (hop + 1) * wide] = jnp.zeros(
                (wide - data, width), BF16
            )

    return pl.pallas_call(
        kernel,
        out_shape=(
            jax.ShapeDtypeStruct((width, wide), BF16),
            jax.ShapeDtypeStruct((width, 2 * wide), BF16),
            jax.ShapeDtypeStruct((1, 3 * wide), F32),
            jax.ShapeDtypeStruct((head_devs * wide, width), BF16),
        ),
        in_specs=[smem()] + vmem(4),
        compiler_params=pltpu.CompilerParams(vmem_limit_bytes=56 * 1024 * 1024),
        name="prepare",
    )(
        head_at.reshape(1),
        qkv_weight,
        out_weight,
        query_bias.reshape(1, width),
        value_bias.reshape(1, width),
    )


def attend(query, blocks, heads, pieces):
    data, wide, _, total_at = lane_plan(heads)
    rows = query.shape[0]
    size = rows // pieces
    count = len(blocks)

    def kernel(*refs):
        query_ref, block_refs = refs[0], refs[1 : 1 + count]
        out_ref, logs_ref = refs[1 + count : 3 + count]
        piece_refs, acc_ref = refs[3 + count : -1], refs[-1]
        acc_ref[...] = jnp.zeros_like(acc_ref)

        def one_head(head):
            own, mask = head_lanes(heads, head)
            query = query_ref[...] * mask
            acc = 0.0
            for ref in block_refs:
                scores = lax.dot_general(query, ref[:, :wide], NT, preferred_element_type=F32)
                weights = jnp.exp(scores).astype(BF16)
                acc = acc + jnp.dot(weights, ref[:, wide:], preferred_element_type=F32)
            total = acc[:, data : data + 1]
            acc_ref[0] += (acc / total) * own
            acc_ref[1] += spread_parts(jnp.log(total), total_at + 3 * head, wide)

        for head in range(heads):
            one_head(head)
        out = acc_ref[0].astype(BF16)
        out_ref[...] = out
        for index, ref in enumerate(piece_refs):
            ref[...] = out[index * size : (index + 1) * size]
        logs_ref[...] = acc_ref[1].astype(BF16)

    shape = jax.ShapeDtypeStruct((rows, wide), BF16)
    small = jax.ShapeDtypeStruct((size, wide), BF16)
    return on_chip(
        kernel, (shape, shape) + (small,) * pieces, [pltpu.VMEM((2, rows, wide), F32)]
    )(query, *blocks)


def project_back(grad, out_rows, pieces):
    rows = grad.shape[0]
    wide = out_rows.shape[0] // pieces

    def kernel(grad_ref, weight_ref, *outs):
        for index, ref in enumerate(outs):
            weight = weight_ref[index * wide : (index + 1) * wide]
            ref[...] = lax.dot_general(
                grad_ref[...], weight, NT, preferred_element_type=F32
            ).astype(BF16)

    return on_chip(kernel, (jax.ShapeDtypeStruct((rows, wide), BF16),) * pieces)(grad, out_rows)


def with_stats(blocks, attended, logs, heads):
    _, wide, delta_at, _ = lane_plan(heads)
    size = blocks[0].shape[0]
    count = len(blocks)

    def kernel(*refs):
        att_ref, logs_ref, out_ref = refs[count:]
        for index, ref in enumerate(refs[:count]):
            at = slice(index * size, (index + 1) * size)
            back = ref[...].astype(F32)
            prod = back * att_ref[at].astype(F32)
            out = back + logs_ref[at].astype(F32)
            for head in range(heads):
                own, _ = head_lanes(heads, head)
                delta = jnp.sum(prod * own, axis=-1, keepdims=True)
                out = out + spread_parts(delta, delta_at + 3 * head, wide)
            out_ref[at] = out.astype(BF16)

    return on_chip(kernel, jax.ShapeDtypeStruct(attended.shape, BF16))(*blocks, attended, logs)


def total_lanes(heads):
    _, wide, _, total_at = lane_plan(heads)
    lane = lax.broadcasted_iota(jnp.int32, (1, wide), 1)
    return ((lane >= total_at) & (lane < total_at + 3 * heads)).astype(BF16)


def query_side(query, back, keyvals, heads):
    _, wide, _, _ = lane_plan(heads)
    rows = query.shape[0]

    def kernel(query_ref, back_ref, *refs):
        keyval_refs, (out_ref, acc_ref) = refs[:-2], refs[-2:]
        acc_ref[...] = jnp.zeros_like(acc_ref)

        def one_head(head, _):
            own, mask = head_lanes(heads, head)
            back_own = back_ref[...] * mask
            query_own = query_ref[...] * mask + back_own * total_lanes(heads)
            acc = 0.0
            for ref in keyval_refs:
                key = ref[:, :wide]
                scores = lax.dot_general(query_own, key, NT, preferred_element_type=F32)
                inner = lax.dot_general(back_own, ref[:, wide:], NT, preferred_element_type=F32)
                half = (jnp.exp(scores) * inner).astype(BF16)
                acc = acc + jnp.dot(half, key, preferred_element_type=F32)
            acc_ref[...] += acc * (own * SCALE)
            return 0

        lax.fori_loop(0, heads, one_head, 0)
        out_ref[...] = acc_ref[...].astype(BF16)

    return on_chip(
        kernel, jax.ShapeDtypeStruct((rows, wide), BF16), [pltpu.VMEM((rows, wide), F32)]
    )(query, back, *keyvals)


def key_side(own, queries, backs, heads):
    _, wide, _, _ = lane_plan(heads)
    rows = queries[0].shape[0]
    count = len(queries)

    def kernel(*refs):
        own_refs, refs = refs[: len(own)], refs[len(own) :]
        query_refs, back_refs = refs[:count], refs[count : 2 * count]
        out_ref, dk_ref, dv_ref = refs[2 * count :]
        keyval = jnp.concatenate([ref[...] for ref in own_refs])
        dk_ref[...] = jnp.zeros_like(dk_ref)
        dv_ref[...] = jnp.zeros_like(dv_ref)

        def one_head(head, _):
            own_lanes, mask = head_lanes(heads, head)
            key_own, value_own = keyval[:, :wide] * mask, keyval[:, wide:] * mask
            dk = dv = 0.0
            for query_ref, back_ref in zip(query_refs, back_refs):
                back_in = back_ref[...]
                query_plain = query_ref[...]
                query = query_plain + back_in * total_lanes(heads)
                scores = lax.dot_general(key_own, query, NT, preferred_element_type=F32)
                probs = jnp.exp(scores)
                inner = lax.dot_general(value_own, back_in, NT, preferred_element_type=F32)
                half = (probs * inner).astype(BF16)
                dv = dv + jnp.dot(probs.astype(BF16), back_in, preferred_element_type=F32)
                dk = dk + jnp.dot(half, query_plain, preferred_element_type=F32)
            dk_ref[...] += dk * own_lanes
            dv_ref[...] += dv * own_lanes
            return 0

        lax.fori_loop(0, heads, one_head, 0)
        out_ref[:, :wide] = dk_ref[...].astype(BF16)
        out_ref[:, wide:] = dv_ref[...].astype(BF16)

    acc = pltpu.VMEM((rows, wide), F32)
    return on_chip(
        kernel, jax.ShapeDtypeStruct((rows, 2 * wide), BF16), [acc, acc]
    )(*own, *queries, *backs)


def weight_rows(grad_query, grad_keyval, rows, attended, grad_rows, core, heads):
    data, wide, _, _ = lane_plan(heads)
    width = rows.shape[1]
    total = 4 * data

    def kernel(core_ref, dq_ref, dkv_ref, rows_ref, att_ref, grad_rows_ref, keep_ref, send_ref, sums_ref, all_ref):
        rows_in = rows_ref[...]
        for slot in range(3):
            part = dq_ref[...] if slot == 0 else dkv_ref[:, (slot - 1) * wide : slot * wide]
            out = lax.dot_general(part, rows_in, TN, preferred_element_type=F32)
            all_ref[slot * data : (slot + 1) * data] = out[:data]
            sums_ref[slot : slot + 1] = jnp.sum(part.astype(F32), axis=0, keepdims=True)
        out = lax.dot_general(
            att_ref[...], grad_rows_ref[...], TN, preferred_element_type=F32
        )
        all_ref[3 * data :] = out[:data]
        half = total // 2
        mine = pl.multiple_of(core_ref[0] * half, 64)
        theirs = pl.multiple_of((1 - core_ref[0]) * half, 64)
        keep_ref[...] = all_ref[pl.ds(mine, half), :]
        send_ref[...] = all_ref[pl.ds(theirs, half), :].astype(BF16)

    return pl.pallas_call(
        kernel,
        out_shape=(
            jax.ShapeDtypeStruct((total // 2, width), F32),
            jax.ShapeDtypeStruct((total // 2, width), BF16),
            jax.ShapeDtypeStruct((3, wide), F32),
        ),
        in_specs=[smem()] + vmem(5),
        scratch_shapes=[pltpu.VMEM((total, width), F32)],
        compiler_params=pltpu.CompilerParams(vmem_limit_bytes=56 * 1024 * 1024),
        name="weight_rows",
    )(core.reshape(1), grad_query, grad_keyval, rows, attended, grad_rows)


def input_rows(grad_query, grad_keyval, q_own, kv_own, pieces):
    width = q_own.shape[0]
    size = grad_query.shape[0] // pieces

    def kernel(dq_ref, dkv_ref, q_ref, kv_ref, *outs):
        query = (dq_ref[...].astype(F32) * (1.0 / SCALE)).astype(BF16)
        out = lax.dot_general(query, q_ref[...], NT, preferred_element_type=F32)
        out = out + lax.dot_general(
            dkv_ref[...], kv_ref[...], NT, preferred_element_type=F32
        )
        out = out.astype(BF16)
        for index, ref in enumerate(outs):
            ref[...] = out[index * size : (index + 1) * size]

    return on_chip(
        kernel, (jax.ShapeDtypeStruct((size, width), BF16),) * pieces
    )(grad_query, grad_keyval, q_own, kv_own)


def assemble(arrays, bits, orders, head_at, head_devs, heads):
    data, _, _, _ = lane_plan(heads)
    width = head_devs * data
    total = 4 * data
    size = total >> len(bits)
    step = 256 if (3 * width) % 256 == 0 else 3 * width
    steps = 3 * width // step

    def kernel(at_ref, *refs):
        ins, (qkv_ref, out_ref, all_ref, turned_ref, sems) = refs[:8], refs[8:]
        own = [at_ref[index] for index in range(len(bits))]
        head = at_ref[len(bits)]
        for number, ref in enumerate(ins):
            side, partner, last = number // 4, number // 2 % 2, number % 2
            halving = orders[side]
            doubling = halving[::-1]
            lanes = slice(side * width // 2, (side + 1) * width // 2)
            for index in range(1 << (len(doubling) - 1)):
                flip = {place: (index >> at) & 1 for at, place in enumerate(doubling[:-1])}
                flip[doubling[-1]] = last
                start = (own[0] ^ partner) * (total // 2)
                for level, place in enumerate(halving):
                    start = start + (own[place] ^ flip[place]) * (total >> (level + 2))
                group = start // data
                within = start - group * data
                for hop_at in range(head_devs):
                    row = group * width + (head ^ hop_at) * data + within
                    from_row = (index * head_devs + hop_at) * size
                    all_ref[pl.ds(pl.multiple_of(row, 8), size), lanes] = ref[
                        from_row : from_row + size
                    ].astype(F32)
        copies = [pltpu.make_async_copy(all_ref.at[pl.ds(3 * width, width)], out_ref, sems.at[0])]
        copies[0].start()
        for index in range(steps):
            at = pl.ds(index * step, step)
            turned_ref[:, at] = all_ref[at].T
            copies.append(
                pltpu.make_async_copy(
                    turned_ref.at[:, at], qkv_ref.at[:, at], sems.at[index + 1]
                )
            )
            copies[-1].start()
        for copy in copies:
            copy.wait()

    return pl.pallas_call(
        kernel,
        out_shape=(
            jax.ShapeDtypeStruct((width, 3 * width), F32),
            jax.ShapeDtypeStruct((width, width), F32),
        ),
        in_specs=[smem()] + vmem(8),
        out_specs=(pl.BlockSpec(memory_space=pl.ANY),) * 2,
        scratch_shapes=[
            pltpu.VMEM((4 * width, width), F32),
            pltpu.VMEM((width, 3 * width), F32),
            pltpu.SemaphoreType.DMA((steps + 1,)),
        ],
        compiler_params=pltpu.CompilerParams(vmem_limit_bytes=56 * 1024 * 1024),
        name="assemble",
    )(jnp.stack(bits + [head_at]).astype(jnp.int32), *arrays)


def bits_of(axis):
    return [(axis, bit) for bit in range(lax.axis_size(axis).bit_length() - 1)]


def bit_value(place):
    axis, bit = place
    return (lax.axis_index(axis) >> bit) & 1


def hop(value, axis, distance):
    return lax.ppermute(value, axis, [(i, i ^ distance) for i in range(lax.axis_size(axis))])


def trade(value, place):
    return hop(value, place[0], 1 << place[1])


def after(value, *others):
    return lax.optimization_barrier((value, *others))[0]


def spread(value):
    high = lax.reduce_precision(value, 8, 7)
    return jnp.concatenate([high, value - high]).astype(BF16)


def halve_message(value, extra, place):
    half = value.shape[0] // 2
    mine = bit_value(place)
    send = lax.dynamic_slice_in_dim(value, (1 - mine) * half, half, 0).astype(BF16)
    keep = lax.dynamic_slice_in_dim(value, mine * half, half, 0)
    return jnp.concatenate([send, spread(extra)]), keep


def halve(value, extra, place):
    message, keep = halve_message(value, extra, place)
    return settle(keep, extra, trade(message, place))


def double(value, place):
    other = trade(value, place)
    first = bit_value(place) == 0
    return jnp.concatenate([jnp.where(first, value, other), jnp.where(first, other, value)])


def settle(keep, extra, got):
    half, count = keep.shape[0], extra.shape[0]
    got = got.astype(F32)
    return (
        keep + got[:half],
        extra + got[half : half + count] + got[half + count :],
    )


def scatter_weight(value):
    for place in bits_of("weight"):
        value = value.reshape((-1, 2) + value.shape[1:])
        mine = bit_value(place)
        send = lax.dynamic_index_in_dim(value, 1 - mine, 1, keepdims=False).astype(BF16)
        keep = lax.dynamic_index_in_dim(value, mine, 1, keepdims=False)
        value = keep + trade(send, place).astype(F32)
    return value[0]


def gather_blocks(value):
    blocks = [value]
    for place in bits_of("weight")[::-1] + bits_of("blk")[1:]:
        blocks = blocks + [trade(block, place) for block in blocks]
    return blocks


def send_head(parts):
    got = [parts[0]]
    for at in range(1, len(parts)):
        got.append(hop(parts[at], "head", at))
    return got


def gather_head(value):
    blocks = {0: value}
    for place in bits_of("head")[::-1]:
        blocks.update(
            {at | 1 << place[1]: trade(each, place) for at, each in blocks.items()}
        )
    return [blocks[at] for at in range(len(blocks))]


def per_device(
    hidden_in,
    qkv_weight,
    query_bias,
    value_bias,
    out_weight,
    out_bias,
    norm1_gain,
    norm1_bias,
    up_weight,
    up_bias,
    down_weight,
    down_bias,
    norm2_gain,
    norm2_bias,
    lengths,
    out_cotangent,
):
    rows_here, _, width = hidden_in.shape
    head_devs = lax.axis_size("head")
    weight_devs = lax.axis_size("weight")
    blk = lax.axis_index("blk")
    head_at = lax.axis_index("head")
    weight_at = lax.axis_index("weight")
    first_seq = (blk & 1) == 0
    heads = HEADS // head_devs
    data, wide, _, _ = lane_plan(heads)
    tokens = 2 * rows_here
    swap = ("blk", 0)

    def to_sequence(value):
        zero, one = value[:, 0], value[:, 1]
        mine = jnp.where(first_seq, zero, one)
        other = trade(jnp.where(first_seq, one, zero), swap)
        return jnp.concatenate([mine, other], axis=0)

    def from_sequence(value, narrow):
        mine = value[:rows_here]
        other = trade(value[rows_here:].astype(narrow), swap).astype(value.dtype)
        return jnp.stack(
            [jnp.where(first_seq, mine, other), jnp.where(first_seq, other, mine)], axis=1
        )

    flat = to_sequence(hidden_in)
    q_own, kv_own, bias_own, out_rows = prepare(
        after(qkv_weight, flat), out_weight, query_bias, value_bias, head_at, head_devs
    )
    hops = gather_head(flat)
    split = head_devs // 2
    near, far = jnp.concatenate(hops[:split]), jnp.concatenate(hops[split:])
    cotangent = to_sequence(after(out_cotangent, flat)).astype(F32)

    def project(part, first):
        index = jnp.arange(part.shape[0], dtype=jnp.int32)
        source = head_at ^ (first + index // tokens)
        within = index % tokens
        source_blk = blk ^ (within // rows_here)
        position = (
            (source_blk * head_devs + source) * weight_devs + weight_at
        ) * rows_here + within % rows_here
        valid = position < jnp.where(first_seq, lengths[0], lengths[1])
        lane = jnp.arange(2 * wide, dtype=jnp.int32)
        masked = jnp.where((lane == data)[None, :] & ~valid[:, None], FAR, 0.0)
        return (
            jnp.dot(part, kv_own, preferred_element_type=F32) + bias_own[:, wide:] + masked
        ).astype(BF16)

    own_keyvals = [project(near, 0), project(far, split)]
    keyvals = gather_blocks(own_keyvals[0])
    keyvals = keyvals + gather_blocks(own_keyvals[1])
    rows = jnp.concatenate([near, far])
    query = (
        jnp.dot(rows, q_own, preferred_element_type=F32) + bias_own[:, :wide]
    ).astype(BF16)
    attended, logs, *parts = attend(query, keyvals, heads, head_devs)
    queries = gather_blocks(after(query, attended))
    returned = send_head(parts)
    returned = jnp.concatenate(returned, axis=1)
    resid1 = flat.astype(F32) + jnp.dot(returned, out_rows, preferred_element_type=F32) + out_bias
    hidden1, normed1, rstd1 = norm_forward(resid1, norm1_gain, norm1_bias)
    gathered = lax.all_gather(hidden1.astype(BF16), "weight", axis=0, tiled=True)
    pre = jnp.dot(gathered, up_weight, preferred_element_type=F32) + up_bias
    active = gelu_value(pre).astype(BF16)
    mixed = scatter_weight(
        jnp.dot(active, down_weight, preferred_element_type=F32).reshape(
            weight_devs, tokens, width
        )
    )
    resid2 = hidden1 + mixed + down_bias
    final, normed2, rstd2 = norm_forward(resid2, norm2_gain, norm2_bias)
    grad_resid2, grad_norm2_gain, grad_norm2_bias = norm_backward(
        cotangent, normed2, rstd2, norm2_gain
    )
    grad_down_bias = jnp.sum(grad_resid2, axis=0)
    mixed_all = lax.all_gather(grad_resid2.astype(BF16), "weight", axis=0, tiled=True)
    grad_pre = lax.dot_general(
        mixed_all, down_weight, NT, preferred_element_type=F32
    ) * gelu_slope(pre)
    grad_up_bias = jnp.sum(grad_pre, axis=0)
    grad_pre_half = grad_pre.astype(BF16)
    back_hidden = scatter_weight(
        lax.dot_general(grad_pre_half, up_weight, NT, preferred_element_type=F32).reshape(
            weight_devs, tokens, width
        )
    )
    grad_down_weight = lax.dot_general(active, mixed_all, TN, preferred_element_type=F32)
    grad_up_weight = lax.dot_general(gathered, grad_pre_half, TN, preferred_element_type=F32)
    up_extra = jnp.pad(grad_up_bias[None], ((0, 7), (0, 0)))
    ffn_keep = jnp.where(first_seq, grad_up_weight, grad_down_weight)
    ffn_send = jnp.concatenate(
        [
            jnp.where(first_seq, grad_down_weight, grad_up_weight).astype(BF16),
            spread(up_extra),
        ]
    )
    grad_hidden1 = grad_resid2 + back_hidden
    grad_resid1, grad_norm1_gain, grad_norm1_bias = norm_backward(
        grad_hidden1, normed1, rstd1, norm1_gain
    )
    grad_out_bias = jnp.sum(grad_resid1, axis=0)
    grad_half, ffn_keep, ffn_send = lax.optimization_barrier(
        (grad_resid1.astype(BF16), ffn_keep, ffn_send)
    )
    ffn_got = trade(ffn_send, swap)
    ffn_places = bits_of("blk")[1:] + bits_of("head")
    layer_out = from_sequence(after(final.astype(BF16), grad_half), BF16)
    backs = project_back(grad_half, out_rows, head_devs)
    backs = send_head(backs)
    back = with_stats(backs, attended, logs, heads)
    back_blocks = gather_blocks(back)
    grad_late = after(grad_half, back)
    grad_rows = jnp.concatenate(
        [grad_late] + [hop(grad_late, "head", at) for at in range(1, head_devs)]
    )
    grad_query = query_side(query, back, keyvals, heads)
    ffn, up_extra = settle(ffn_keep, up_extra, after(ffn_got, grad_query))
    ffn_message, ffn_keep = halve_message(ffn, up_extra, ffn_places[0])
    ffn_got = trade(ffn_message, ffn_places[0])
    grad_keyval = key_side(own_keyvals, queries, back_blocks, heads)
    ffn, up_extra = settle(ffn_keep, up_extra, after(ffn_got, grad_keyval))
    for place in ffn_places[1:]:
        ffn, up_extra = halve(ffn, up_extra, place)
    ffn = ffn.astype(BF16)

    weight_bits, blk_bits = bits_of("weight"), bits_of("blk")
    core, middle, outer = weight_bits[0], weight_bits[1:], blk_bits
    keep, send, column_sums = weight_rows(
        grad_query, grad_keyval, rows, attended, grad_rows, bit_value(core), heads
    )
    column_sums = column_sums[:, :data]
    bias_rows = lax.dynamic_update_slice(
        jnp.zeros((2, head_devs, data), F32),
        jnp.stack([column_sums[0], column_sums[2]])[:, None],
        (0, head_at, 0),
    ).reshape(2, width)
    extra = jnp.concatenate(
        [
            bias_rows,
            jnp.stack([
                grad_out_bias,
                grad_norm1_gain,
                grad_norm1_bias,
                grad_norm2_gain,
                grad_norm2_bias,
                grad_down_bias,
            ]),
        ]
    )
    count = extra.shape[0]
    got = trade(jnp.concatenate([send, spread(extra)]), core)
    value, extra = settle(keep, extra, got)
    lane_half = width // 2
    orders = (middle + outer, outer + middle)
    sides = [
        (value[:, at * lane_half : (at + 1) * lane_half], extra[:, at * lane_half : (at + 1) * lane_half])
        for at in range(2)
    ]
    for level in range(len(middle + outer)):
        out = [halve_message(*sides[at], orders[at][level]) for at in range(2)]
        messages = lax.optimization_barrier((out[0][0], out[1][0]))
        got = [trade(messages[at], orders[at][level]) for at in range(2)]
        sides = [settle(out[at][1], sides[at][1], got[at]) for at in range(2)]
    sides = [jnp.concatenate([part.astype(BF16), spread(small)]) for part, small in sides]
    piece = jnp.concatenate(sides, axis=1)
    partial = input_rows(grad_query, grad_keyval, q_own, kv_own, head_devs)
    piece, *partial = lax.optimization_barrier((piece, *partial))
    pieces = gather_head(piece)
    size = piece.shape[0] - 2 * count
    small = sum(
        each[size : size + count].astype(F32) + each[size + count :].astype(F32)
        for each in pieces
    )
    stacked = jnp.concatenate([each[:size] for each in pieces])
    for place in ffn_places[:0:-1]:
        ffn = double(ffn, place)
    left, right = ffn[:, :lane_half], ffn[:, lane_half:]
    first_row = bit_value(ffn_places[0]) == 0

    def in_order(first, mine, other):
        return jnp.where(first, mine, other), jnp.where(first, other, mine)

    left_got, right_got = trade(left, ffn_places[0]), trade(right, swap)
    left = jnp.concatenate(in_order(first_row, left, left_got))
    right = jnp.concatenate(in_order(first_seq, right, right_got))
    left_got, right_got = trade(left, swap), trade(right, ffn_places[0])
    half_rows = right.shape[0] // 2
    up_left, down_left = in_order(first_seq, left, left_got)
    up_right = jnp.concatenate(in_order(first_row, right[:half_rows], right_got[:half_rows]))
    down_right = jnp.concatenate(in_order(first_row, right[half_rows:], right_got[half_rows:]))
    sides = [stacked[:, :lane_half], stacked[:, lane_half:]]
    count = len(middle + outer)
    for level in range(count - 1):
        got = [trade(sides[at], orders[at][::-1][level]) for at in range(2)]
        sides = [jnp.concatenate([sides[at], got[at]]) for at in range(2)]
    last = [trade(sides[at], orders[at][0]) for at in range(2)]
    arrays = [
        each
        for at in range(2)
        for each in (sides[at], last[at], trade(sides[at], core), trade(last[at], core))
    ]
    slot = {place: at for at, place in enumerate([core] + middle + outer)}
    grad_qkv_weight, grad_out_weight = assemble(
        arrays,
        [bit_value(place) for place in [core] + middle + outer],
        [[slot[at] for at in order] for order in orders],
        head_at,
        head_devs,
        heads,
    )

    partial = lax.optimization_barrier((*partial, stacked))[:-1]
    grad_in = grad_resid1 + partial[0].astype(F32)
    for at in range(1, head_devs):
        part = hop(partial[at], "head", at)
        grad_in = grad_in + part.astype(F32)
    grad_in = from_sequence(grad_in, BF16)
    return (
        layer_out,
        grad_in,
        grad_qkv_weight,
        small[0],
        small[1],
        grad_out_weight,
        small[2],
        small[3],
        small[4],
        jnp.concatenate([up_left, up_right], axis=1).astype(F32),
        up_extra[0],
        jnp.concatenate([down_left, down_right], axis=1).astype(F32),
        small[7],
        small[5],
        small[6],
    )


def solution(mesh):
    placed = (
        P(("blk", "head", "weight"), None, None),
        P(),
        P(),
        P(),
        P(),
        P(),
        P(),
        P(),
        P(None, "weight"),
        P("weight"),
        P("weight", None),
        P(),
        P(),
        P(),
        P(),
        P(("blk", "head", "weight"), None, None),
    )

    return jax.shard_map(
        per_device,
        mesh=mesh,
        in_specs=placed,
        out_specs=(
            P(("blk", "head", "weight"), None, None),
            P(("blk", "head", "weight"), None, None),
            P(),
            P(),
            P(),
            P(),
            P(),
            P(),
            P(),
            P(None, "weight"),
            P("weight"),
            P("weight", None),
            P(),
            P(),
            P(),
        ),
        check_vma=False,
    )
```
